256 devices in a mesh: pass: 32 (over x, y, core), kv: 8 (over z).
Axes of the slice: x: 4, y: 4, z: 8, core: 2. Of those that a mesh axis runs over, the one named last changes fastest.
Arguments:
- queries: bfloat16 [32, 64, 8192], P('pass', None, 'kv'), may hold values from -40 to 40
- suffix_keys: bfloat16 [32, 64, 1024], P('pass', None, 'kv'), may hold values from -5 to 5
- suffix_values: bfloat16 [32, 64, 1024], P('pass', None, 'kv'), may hold values from -40 to 40
- passage_keys: bfloat16 [128, 1024, 1024], P('pass', None, 'kv'), may hold values from -5 to 5
- passage_values: bfloat16 [128, 1024, 1024], P('pass', None, 'kv'), may hold values from -40 to 40
- fresh_keys: bfloat16 [32, 8, 128, 1024], P('pass', None, None, 'kv'), may hold values from -5 to 5
- fresh_values: bfloat16 [32, 8, 128, 1024], P('pass', None, None, 'kv'), may hold values from -40 to 40
- citations: int32 [32, 8], P('pass'), may hold values from 0 to 127, all different within a row; in each aligned block of 32 rows (0 to 31, 32 to 63, ...) at most 4 rows name the same one
- selected: int32 [32, 8, 128], P('pass'), may hold values from 0 to 1023, as said below
Outputs:
- attention: bfloat16 [32, 64, 8192], P('pass', 'kv')
The draws below stay inside these ranges and needn't reach their ends.
Inputs may be any that keep to these rules, and one draw needn't show every extreme that they name: `citations`: each request cites 8 distinct passages; every passage is cited; no passage is cited by more than 4 requests, a bound that some block reaches. `selected`: each list holds 128 distinct positions of its passage.
All inputs are finite; a program needn't handle non-finite values.
Results may differ from the reference program's by a relative error of at most 0.0053.
Values may be sent and summed in bfloat16 or wider, within the bound.
No kernel may reach another device: no remote copies, remote signals or barrier semaphores. Data moves between devices by JAX's collectives and lax.ppermute only.
A program may use at most 128 MiB of HBM per device.

```python
import math
import jax
import jax.numpy as jnp
import numpy as np
from jax import lax

HD = 128
GROUP = 8
L = 1024
CITE = 8
SEL = 128
S = 64
PASS_DEV = 4
PMOST = 4
KVH = 8
REQ = 32
PASSAGES = 128


def suffix_pair(key):
    key_rows = jnp.clip(jax.random.normal(jax.random.fold_in(key, 11), (REQ, S, KVH, HD), jnp.float32), -5.0, 5.0)
    query_rows = 1.5 * jnp.clip(jax.random.normal(jax.random.fold_in(key, 12), (REQ, S, KVH, GROUP, HD), jnp.float32), -5.0, 5.0)
    return (query_rows.reshape(REQ, S, KVH * GROUP * HD), key_rows.reshape(REQ, S, KVH * HD))


def draw_queries(key, part):
    return suffix_pair(key)[0].astype(jnp.bfloat16)


def draw_suffix_keys(key, part):
    return suffix_pair(key)[1].astype(jnp.bfloat16)


def draw_passage_keys(key, part):
    rows = jnp.clip(jax.random.normal(jax.random.fold_in(key, 41), (PASSAGES, L, KVH, HD), jnp.float32), -5.0, 5.0)
    return rows.reshape(PASSAGES, L, KVH * HD).astype(jnp.bfloat16)


def draw_selected(key, part):
    base_key = jax.random.fold_in(key, 21)
    row_keys = jax.random.split(base_key, REQ * CITE)
    picked = jax.vmap(lambda row_key: jax.random.permutation(row_key, L)[:SEL])(row_keys)
    return picked.reshape(REQ, CITE, SEL).astype(jnp.int32)


def block_scale(stream_key, shape, cuts, low, top_value):
    def one(position, blocks):
        steps = jax.random.uniform(jax.random.fold_in(jax.random.fold_in(stream_key, 6), position), (blocks,), jnp.float32, low / len(cuts), top_value / len(cuts))
        return jnp.repeat(jnp.exp(steps), shape[position] // blocks).reshape((-1,) + (1,) * (len(shape) - position - 1))

    level = one(*cuts[0])
    for cut in cuts[1:]:
        level = level * one(*cut)
    return level


def shared_out(stream_key, own, number, rows, number_of, top, reach, lean):
    ranking = jax.random.permutation(stream_key, number_of)
    crowded, usual = load_shares(number_of, rows * top, reach, lean, True), load_shares(number_of, rows * top, reach, lean, False)
    places = jnp.arange(number_of)

    def named(lengths, rotation):
        used = int((lengths > 0).sum())
        fixed = max(1, used // 4)
        moved = fixed + (places - fixed + rotation * (used - fixed)) % max(1, number_of - fixed)
        return jnp.zeros((number_of,), jnp.int32).at[ranking[jnp.where(places < fixed, places, moved)]].set(jnp.asarray(lengths, jnp.int32))

    lengths = jnp.where(number % 4 == 0, named(crowded, number // 4), named(usual, number - number // 4 - 1))
    mixed = jax.random.permutation(jax.random.fold_in(own, 3), number_of)
    donor, sink = mixed[0:number_of // 2 * 2:2], mixed[1:number_of // 2 * 2:2]
    room = jnp.minimum(lengths[donor] - 1, reach - lengths[sink]) // 2
    room = jnp.where((donor == ranking[0]) | (sink == ranking[0]) | (lengths[sink] == 0), 0, jnp.maximum(room, 0))
    moved = jax.random.randint(jax.random.fold_in(own, 4), (number_of // 2,), 0, 1 << 20) % (room + 1)
    lengths = lengths.at[donor].add(-moved).at[sink].add(moved)
    labels = jnp.searchsorted(jnp.cumsum(lengths), jnp.arange(rows * top), side="right").astype(jnp.int32)
    grid = labels.reshape(top, rows).T
    grid = grid[jax.random.permutation(jax.random.fold_in(own, 1), rows)]
    rotation = jax.random.randint(jax.random.fold_in(own, 2), (rows, 1), 0, top)
    return jnp.take_along_axis(grid, (jnp.arange(top)[None, :] + rotation) % top, axis=1)


def load_shares(count, total, limit, slope, full):
    portions = [(1 << 20) // math.isqrt(standing ** slope) + 1 for standing in range(1, count + 1)]
    largest = limit if full else min(limit, max(-(-total // count), total * portions[0] // sum(portions)))
    least = 1 if total - largest >= count - 1 else 0
    given, spare = [largest] + [least] * (count - 1), total - largest - least * (count - 1)
    while spare > 0:
        candidates = [i for i in range(1, count) if given[i] < largest] or [i for i in range(1, count) if given[i] < limit]
        pool, remaining = sum([portions[i] for i in candidates]), spare
        for i in candidates:
            more = min(limit - given[i], max(1, remaining * portions[i] // pool), spare)
            given[i] = given[i] + more
            spare = spare - more
    return np.array(given)


def bell_draw(rng, extent, width, reach, shards=(), held_as=jnp.bfloat16):
    values = jax.random.normal(rng, extent, jnp.float32) * width
    if len(shards) > 0:
        values = block_scale(rng, extent, shards, -0.22, 0.18) * values
    return jnp.clip(values, min=-reach, max=reach).astype(held_as)


def setup_inputs(seed: int = 0) -> dict:
    key_list = jax.random.split(jax.random.key(seed), 10)
    queries = draw_queries(jax.random.fold_in(key_list[9], 71), 0)
    suffix_keys = draw_suffix_keys(jax.random.fold_in(key_list[9], 71), 0)
    suffix_values = bell_draw(key_list[2], (REQ, S, KVH * HD), 8.0, 40.0, ((0, 32), (2, 8)))
    passage_keys = draw_passage_keys(jax.random.fold_in(key_list[9], 71), 0)
    passage_values = bell_draw(key_list[4], (PASSAGES, L, KVH * HD), 8.0, 40.0, ((0, 32), (2, 8)))
    fresh_keys = bell_draw(key_list[5], (REQ, CITE, SEL, KVH * HD), 1.0, 5.0, ((0, 32), (3, 8)))
    fresh_values = bell_draw(key_list[6], (REQ, CITE, SEL, KVH * HD), 8.0, 40.0, ((0, 32), (3, 8)))
    citations_keys = jax.random.split(jax.random.fold_in(key_list[7], 1), REQ // REQ)
    citations_turns = jax.random.permutation(jax.random.fold_in(key_list[7], 3), REQ // REQ)
    citations = jax.vmap(lambda own, number: shared_out(jax.random.fold_in(key_list[7], 2), own, number, REQ, PASSAGES, CITE, PMOST, 2))(citations_keys, citations_turns).reshape((REQ, CITE))
    selected = draw_selected(jax.random.fold_in(key_list[9], 71), 0)
    return dict(queries=queries, suffix_keys=suffix_keys, suffix_values=suffix_values, passage_keys=passage_keys, passage_values=passage_values, fresh_keys=fresh_keys, fresh_values=fresh_values, citations=citations, selected=selected)


very_low = -1e+30

def rounded_float(array):
    return lax.optimization_barrier(array.astype(jnp.bfloat16)).astype(jnp.float32)

def reference(queries, suffix_keys, suffix_values, passage_keys, passage_values, fresh_keys, fresh_values, citations, selected):
    score_scale = 1.0 / math.sqrt(HD)
    cite_ids = jnp.arange(CITE, dtype=jnp.int32)
    positions = jnp.arange(L, dtype=jnp.int32)
    host_span = S + CITE * SEL
    later = jnp.arange(host_span, dtype=jnp.int32)[None, :]
    causal = (later >= S) | (later <= jnp.arange(S, dtype=jnp.int32)[:, None])
    highest = lax.Precision.HIGHEST

    def one_request(packed):
        query_rows, own_keys, own_values, new_keys, new_values, cite_row, pick_rows = packed
        query_float = query_rows.astype(jnp.float32).reshape(S, KVH, GROUP, HD)
        cached_keys = passage_keys[cite_row].astype(jnp.float32).reshape(CITE, L, KVH, HD)
        cached_values = passage_values[cite_row].astype(jnp.float32).reshape(CITE, L, KVH, HD)
        dropped = jnp.any(pick_rows[:, :, None] == positions[None, None, :], axis=1)
        scores = jnp.einsum('skgd,clkd->ckgsl', query_float, cached_keys, precision=highest) * score_scale
        scores = jnp.where(dropped[:, None, None, None, :], very_low, scores)
        cite_max = lax.optimization_barrier(jnp.max(scores, axis=-1))
        owner_ids = cite_row // PASS_DEV
        same_group = owner_ids[:, None] == owner_ids[None, :]
        group_max = lax.optimization_barrier(jnp.max(jnp.where(same_group[:, :, None, None, None], cite_max[None], very_low), axis=1))
        weights = jnp.exp(scores - group_max[..., None])
        same_float = same_group.astype(jnp.float32)
        group_sum = jnp.einsum('ab,bkgs->akgs', same_float, lax.optimization_barrier(jnp.sum(weights, axis=-1)), precision=highest)
        cite_acc = jnp.einsum('ckgsl,clkd->ckgsd', rounded_float(weights), cached_values, precision=highest)
        group_acc = jnp.einsum('ab,bkgsd->akgsd', same_float, cite_acc, precision=highest)
        group_out = rounded_float(group_acc / group_sum[..., None])
        earlier = same_group & (cite_ids[None, :] < cite_ids[:, None])
        leading = jnp.logical_not(jnp.any(earlier, axis=1))
        host_keys = jnp.concatenate([own_keys, new_keys.reshape(CITE * SEL, KVH * HD)], axis=0).astype(jnp.float32).reshape(host_span, KVH, HD)
        host_values = jnp.concatenate([own_values, new_values.reshape(CITE * SEL, KVH * HD)], axis=0).astype(jnp.float32).reshape(host_span, KVH, HD)
        host_scores = jnp.einsum('skgd,tkd->kgst', query_float, host_keys, precision=highest) * score_scale
        host_scores = jnp.where(causal[None, None], host_scores, very_low)
        host_max = lax.optimization_barrier(jnp.max(host_scores, axis=-1))
        host_weights = jnp.exp(host_scores - host_max[..., None])
        host_sum = lax.optimization_barrier(jnp.sum(host_weights, axis=-1))
        host_acc = jnp.einsum('kgst,tkd->kgsd', rounded_float(host_weights), host_values, precision=highest)
        ceiling = jnp.maximum(host_max, lax.optimization_barrier(jnp.max(group_max, axis=0)))
        shares = jnp.where(leading[:, None, None, None], group_sum * jnp.exp(group_max - ceiling[None]), 0.0)
        near_scale = jnp.exp(host_max - ceiling)
        numerator = host_acc * near_scale[..., None] + lax.optimization_barrier(jnp.sum(shares[..., None] * group_out, axis=0))
        denominator = host_sum * near_scale + lax.optimization_barrier(jnp.sum(shares, axis=0))
        result = numerator / denominator[..., None]
        return result.transpose(2, 0, 1, 3).reshape(S, KVH * GROUP * HD).astype(jnp.bfloat16)
    return lax.map(one_request, (queries, suffix_keys, suffix_values, fresh_keys, fresh_values, citations, selected))
```

```python
import functools
import math

import jax
import jax.numpy as jnp
from jax import lax
from jax.experimental import pallas as pl
from jax.experimental.pallas import tpu as pltpu
from jax.sharding import Mesh
from jax.sharding import PartitionSpec as P

HD = 128
LANES = 128
PARTS = 3
RING = 4
HOPS = (0, 1, 3, 2)
very_low = -1e30
log2_scale = math.log2(math.e) / math.sqrt(HD)
VMEM_BYTES = 48 * 1024 * 1024


def contract_last(left, right):
    return lax.dot_general(
        left, right, (((1,), (1,)), ((), ())), preferred_element_type=jnp.float32
    )


def stack_heads(rows, heads):
    return jnp.concatenate([rows[:, g * HD : (g + 1) * HD] for g in range(heads)], axis=0)


def attend_kernel(
    table_ref, packed_ref, key_ref, value_ref, out_ref, mask_s, query_s, max_s, acc_s, *, suffix_len, heads, cites
):
    rows = suffix_len * heads
    chunk = rows // 2
    requests = packed_ref.shape[0]
    mask_s[...] = packed_ref[:, suffix_len : suffix_len + cites, :].astype(jnp.float32)

    def one_request(j, carry):
        query_s[...] = stack_heads(packed_ref[j, 0:suffix_len, :], heads)
        max_s[...] = jnp.full_like(max_s, very_low)
        acc_s[...] = jnp.zeros_like(acc_s)

        def one_cite(c, inner):
            place = table_ref[j, c]

            @pl.when(place >= 0)
            def _():
                bias = mask_s[j, pl.ds(c, 1), :]
                for start in range(0, rows, chunk):
                    part = pl.ds(start, chunk)
                    scores = contract_last(query_s[part, :], key_ref[place]) * log2_scale + bias
                    old_max = max_s[part, :]
                    new_max = jnp.maximum(old_max, jnp.max(scores, axis=1, keepdims=True))
                    weights = jnp.exp2(scores - new_max[:, 0:1]).astype(jnp.bfloat16)
                    factor = jnp.exp2(old_max - new_max)
                    added = jnp.dot(weights, value_ref[place], preferred_element_type=jnp.float32)
                    acc_s[part, :] = acc_s[part, :] * jnp.concatenate([factor, factor], axis=1) + added
                    max_s[part, :] = new_max

            return inner

        lax.fori_loop(0, cites, one_cite, 0)
        lane = lax.broadcasted_iota(jnp.int32, (suffix_len, LANES), 1)
        stats = jnp.zeros((suffix_len, LANES), jnp.float32)
        for g in range(heads):
            part = slice(g * suffix_len, (g + 1) * suffix_len)
            total = acc_s[part, HD : 2 * HD]
            live = total > 0.0
            safe = jnp.where(live, total, 1.0)
            out_ref[j, :, g * HD : (g + 1) * HD] = (acc_s[part, 0:HD] / safe).astype(jnp.bfloat16)
            level = jnp.where(live, max_s[part, :] + jnp.log2(safe), very_low)
            stats = put_level(stats, level, lane, g, heads)
        out_ref[j, :, heads * HD :] = stats.astype(jnp.bfloat16)
        return carry

    lax.fori_loop(0, requests, one_request, 0)


def put_level(stats, level, lane, g, heads):
    for i in range(PARTS):
        piece = level.astype(jnp.bfloat16).astype(jnp.float32)
        stats = jnp.where(lane == i * heads + g, piece, stats)
        level = level - piece
    return stats


def get_level(tile, heads):
    level = tile.astype(jnp.float32)
    total = level
    for i in range(1, PARTS):
        total = total + pltpu.roll(level, LANES - i * heads, 1)
    return total


def host_kernel(query_ref, fresh_key_ref, fresh_value_ref, suffix_key_ref, suffix_value_ref, out_ref, level_ref):
    suffix_len, width = query_ref.shape
    heads = width // HD
    query = stack_heads(query_ref[...], heads)
    fresh = contract_last(query, fresh_key_ref[...]) * log2_scale
    near = contract_last(query, suffix_key_ref[...]) * log2_scale
    place = lax.broadcasted_iota(jnp.int32, near.shape, 0) % suffix_len
    near = jnp.where(lax.broadcasted_iota(jnp.int32, near.shape, 1) <= place, near, very_low)
    top = jnp.maximum(jnp.max(fresh, axis=1, keepdims=True), jnp.max(near, axis=1, keepdims=True))
    fresh = jnp.exp2(fresh - top)
    near = jnp.exp2(near - top)
    total = jnp.sum(fresh, axis=1, keepdims=True) + jnp.sum(near, axis=1, keepdims=True)
    acc = jnp.dot(fresh.astype(jnp.bfloat16), fresh_value_ref[...], preferred_element_type=jnp.float32)
    acc = acc + jnp.dot(near.astype(jnp.bfloat16), suffix_value_ref[...], preferred_element_type=jnp.float32)
    acc = acc / total
    level = jnp.broadcast_to(top + jnp.log2(total), acc.shape)
    lane = lax.broadcasted_iota(jnp.int32, (suffix_len, LANES), 1)
    levels = jnp.zeros((suffix_len, LANES), jnp.float32)
    for g in range(heads):
        part = slice(g * suffix_len, (g + 1) * suffix_len)
        out_ref[:, g * HD : (g + 1) * HD] = acc[part]
        levels = jnp.where(lane == g, level[part], levels)
    level_ref[...] = levels


def weigh(levels):
    top = functools.reduce(jnp.maximum, levels)
    shares = [jnp.exp2(level - top) for level in levels]
    total = functools.reduce(jnp.add, shares)
    return [share / total for share in shares], top + jnp.log2(total)


def merge_kernel(*refs):
    sources, out_ref = refs[:-1], refs[-1]
    requests, suffix_len, wide = out_ref.shape
    heads = (wide - LANES) // HD
    lane = lax.broadcasted_iota(jnp.int32, (suffix_len, LANES), 1)
    for j in range(requests):
        shares, level = weigh([get_level(s[j, :, heads * HD :], heads) for s in sources])
        for g in range(heads):
            part = slice(g * HD, (g + 1) * HD)
            terms = [s[j, :, part].astype(jnp.float32) * w[:, g : g + 1] for s, w in zip(sources, shares)]
            out_ref[j, :, part] = functools.reduce(jnp.add, terms).astype(jnp.bfloat16)
        stats = jnp.zeros((suffix_len, LANES), jnp.float32)
        for i in range(PARTS):
            piece = level.astype(jnp.bfloat16).astype(jnp.float32)
            moved = piece if i == 0 else pltpu.roll(piece, i * heads, 1)
            stats = jnp.where((lane >= i * heads) & (lane < (i + 1) * heads), moved, stats)
            level = level - piece
        out_ref[j, :, heads * HD :] = stats.astype(jnp.bfloat16)


def final_kernel(*refs):
    sources, host_ref, level_ref, out_ref = refs[:-3], refs[-3], refs[-2], refs[-1]
    suffix_len, width = out_ref.shape
    heads = width // HD
    levels = [get_level(s[:, width:], heads) for s in sources] + [level_ref[...]]
    shares, _ = weigh(levels)
    for g in range(heads):
        part = slice(g * HD, (g + 1) * HD)
        terms = [s[:, part].astype(jnp.float32) * w[:, g : g + 1] for s, w in zip(sources, shares)]
        terms.append(host_ref[:, part] * shares[-1][:, g : g + 1])
        out_ref[:, part] = functools.reduce(jnp.add, terms).astype(jnp.bfloat16)


def in_vmem(kernel, out_shape, operands, scratch=(), smem=0, name=None):
    spaces = [pltpu.SMEM] * smem + [pltpu.VMEM] * (len(operands) - smem)
    many = isinstance(out_shape, tuple)
    return pl.pallas_call(
        kernel,
        out_shape=out_shape,
        in_specs=[pl.BlockSpec(memory_space=s) for s in spaces],
        out_specs=tuple(pl.BlockSpec(memory_space=pltpu.VMEM) for _ in out_shape)
        if many
        else pl.BlockSpec(memory_space=pltpu.VMEM),
        scratch_shapes=list(scratch),
        compiler_params=pltpu.CompilerParams(vmem_limit_bytes=VMEM_BYTES),
        name=name,
    )(*operands)


def shift(value, axis, hop):
    return lax.ppermute(value, axis, [(i, (i + hop) % RING) for i in range(RING)])


def body(
    queries,
    suffix_keys,
    suffix_values,
    passage_keys,
    passage_values,
    fresh_keys,
    fresh_values,
    citations,
    selected,
):
    _, suffix_len, width = queries.shape
    local_passages, length, _ = passage_keys.shape
    heads = width // HD
    cites = citations.shape[1]
    chip = lax.axis_index("x") * RING + lax.axis_index("y")
    core = lax.axis_index("c")

    positions = jnp.arange(length, dtype=jnp.int32)
    dropped = jnp.any(selected[0][:, :, None] == positions[None, None, :], axis=1)
    masks = jnp.where(dropped, very_low, 0.0).astype(jnp.bfloat16)
    ids = jnp.pad(citations.astype(jnp.bfloat16), ((0, 7), (0, width - cites)))
    packed = jnp.concatenate([queries[0], masks, ids], axis=0)

    swap = [(0, 1), (1, 0)]
    keys = jnp.concatenate([passage_keys, lax.ppermute(passage_keys, "c", swap)], axis=0)
    values = jnp.concatenate([passage_values, lax.ppermute(passage_values, "c", swap)], axis=0)
    values = jnp.concatenate([values, jnp.ones_like(values)], axis=2)

    row = jnp.stack([packed] + [shift(packed, "x", hop) for hop in HOPS[1:]])
    classes = [row] + [shift(row, "y", hop) for hop in HOPS[1:]]

    host_out, host_level = in_vmem(
        host_kernel,
        (
            jax.ShapeDtypeStruct((suffix_len, width), jnp.float32),
            jax.ShapeDtypeStruct((suffix_len, LANES), jnp.float32),
        ),
        (
            queries[0],
            fresh_keys.reshape(-1, HD),
            fresh_values.reshape(-1, HD),
            suffix_keys[0],
            suffix_values[0],
        ),
        name="host_part",
    )

    rows = suffix_len * heads
    results = []
    for block in classes:
        named = block[:, suffix_len + cites, 0:cites].astype(jnp.int32)
        local = named - chip * (2 * local_passages)
        here = (local >= 0) & (local < 2 * local_passages)
        table = jnp.where(here, (local + core * local_passages) % (2 * local_passages), -1)
        results.append(
            in_vmem(
                functools.partial(attend_kernel, suffix_len=suffix_len, heads=heads, cites=cites),
                jax.ShapeDtypeStruct((RING, suffix_len, width + LANES), jnp.bfloat16),
                (table, block, keys, values),
                scratch=(
                    pltpu.VMEM((RING, cites, length), jnp.float32),
                    pltpu.VMEM((rows, HD), jnp.bfloat16),
                    pltpu.VMEM((rows, LANES), jnp.float32),
                    pltpu.VMEM((rows, 2 * HD), jnp.float32),
                ),
                smem=1,
                name="attend_class",
            )
        )
    back = [results[0]] + [shift(r, "y", RING - hop) for r, hop in zip(results[1:], HOPS[1:])]
    merged = in_vmem(
        merge_kernel,
        jax.ShapeDtypeStruct((RING, suffix_len, width + LANES), jnp.bfloat16),
        tuple(back),
        name="merge_row",
    )
    home = [merged[0]] + [shift(merged[j], "x", RING - HOPS[j]) for j in range(1, RING)]
    attended = in_vmem(
        final_kernel,
        jax.ShapeDtypeStruct((suffix_len, width), jnp.bfloat16),
        tuple(home) + (host_out, host_level),
        name="merge_home",
    )
    groups = lax.psum(1, "kv")
    pieces = attended.reshape(groups, suffix_len // groups, width)
    pieces = lax.all_to_all(pieces, "kv", split_axis=0, concat_axis=0, tiled=True)
    return jnp.transpose(pieces, (1, 0, 2)).reshape(1, suffix_len // groups, groups * width)


def solution(mesh):
    fine = Mesh(mesh.devices.reshape(RING, RING, 2, -1), ("x", "y", "c", "kv"))
    part = ("x", "y", "c")
    placed = (
        P(part, None, "kv"),
        P(part, None, "kv"),
        P(part, None, "kv"),
        P(part, None, "kv"),
        P(part, None, "kv"),
        P(part, None, None, "kv"),
        P(part, None, None, "kv"),
        P(part, None),
        P(part, None, None),
    )
    return jax.shard_map(body, mesh=fine, in_specs=placed, out_specs=P(part, "kv", None), check_vma=False)
```

```python
import functools
import math

import jax
import jax.numpy as jnp
from jax import lax
from jax.experimental import pallas as pl
from jax.experimental.pallas import tpu as pltpu
from jax.sharding import Mesh
from jax.sharding import PartitionSpec as P

HD = 128
LANES = 128
PARTS = 3
RING = 4
HOPS = (0, 1, 3, 2)
very_low = -1e30
log2_scale = math.log2(math.e) / math.sqrt(HD)
VMEM_BYTES = 24 * 1024 * 1024


def contract_last(left, right):
    return lax.dot_general(
        left, right, (((1,), (1,)), ((), ())), preferred_element_type=jnp.float32
    )


def stack_heads(rows, heads):
    return jnp.concatenate([rows[:, g * HD : (g + 1) * HD] for g in range(heads)], axis=0)


def pack_kernel(cite_ref, query_ref, picks_ref, out_ref, sem):
    suffix_len, width = query_ref.shape
    cites, pick_count = picks_ref.shape
    blocks = width // LANES
    copy = pltpu.make_async_copy(query_ref, out_ref.at[pl.ds(0, suffix_len), :], sem)
    copy.start()
    picks = jnp.concatenate([picks_ref[c : c + 1, :] for c in range(cites)], axis=1)
    total = cites * pick_count
    within = lax.broadcasted_iota(jnp.int32, (LANES, total), 0)
    low = jnp.where(within == picks % LANES, 1.0, 0.0).astype(jnp.bfloat16)
    row = lax.broadcasted_iota(jnp.int32, (blocks * cites, total), 0)
    owner = lax.broadcasted_iota(jnp.int32, (blocks * cites, total), 1) // pick_count
    high = jnp.where(row == (picks // LANES) * cites + owner, 1.0, 0.0).astype(jnp.bfloat16)
    hits = contract_last(high, low)
    line = lax.broadcasted_iota(jnp.int32, (cites, LANES), 0)
    ids = jnp.zeros((cites, LANES), jnp.int32)
    for c in range(cites):
        ids = jnp.where(line == c, cite_ref[0, c], ids)
    ids = ids.astype(jnp.float32)
    for h in range(blocks):
        hit = hits[h * cites : (h + 1) * cites, :]
        out_ref[suffix_len:, h * LANES : (h + 1) * LANES] = jnp.where(hit > 0.5, -1.0 - ids, ids).astype(jnp.bfloat16)
    copy.wait()


def row_kernel(*refs):
    for j, source in enumerate(refs[:-1]):
        refs[-1][j, :, :] = source[...]


def attend_kernel(*refs, count, suffix_len, heads, cites):
    tables, blocks = refs[0:count], refs[count : 2 * count]
    own_key, own_value, other_key, other_value = refs[2 * count : 2 * count + 4]
    outs = refs[2 * count + 4 : 3 * count + 4]
    mask_s, query_s, max_s, acc_s = refs[3 * count + 4 :]
    rows = suffix_len * heads
    chunk = rows // 2
    requests = blocks[0].shape[0]
    local = own_key.shape[0]

    def add_slot(key_ref, value_ref, place, bias):
        for start in range(0, rows, chunk):
            part = pl.ds(start, chunk)
            scores = contract_last(query_s[part, :], key_ref[place]) * log2_scale + bias
            old_max = max_s[part, :]
            new_max = jnp.maximum(old_max, jnp.max(scores, axis=1, keepdims=True))
            weights = jnp.exp2(scores - new_max[:, 0:1]).astype(jnp.bfloat16)
            factor = jnp.exp2(old_max - new_max)
            value = value_ref[place]
            value = jnp.concatenate([value, jnp.ones_like(value)], axis=1)
            added = jnp.dot(weights, value, preferred_element_type=jnp.float32)
            acc_s[part, :] = acc_s[part, :] * jnp.concatenate([factor, factor], axis=1) + added
            max_s[part, :] = new_max

    for table_ref, packed_ref, out_ref in zip(tables, blocks, outs):

        def one_request(j, carry):
            found = table_ref[j, 0]
            for c in range(1, cites):
                found = jnp.maximum(found, table_ref[j, c])

            @pl.when(found >= 0)
            def _():
                query_s[...] = stack_heads(packed_ref[j, 0:suffix_len, :], heads)
                marks = packed_ref[j, suffix_len : suffix_len + cites, :].astype(jnp.float32)
                mask_s[...] = jnp.where(marks < 0.0, very_low, 0.0)
                max_s[...] = jnp.full_like(max_s, very_low)
                acc_s[...] = jnp.zeros_like(acc_s)

                def one_cite(c, inner):
                    place = table_ref[j, c]

                    @pl.when((place >= 0) & (place < local))
                    def _():
                        add_slot(own_key, own_value, place, mask_s[pl.ds(c, 1), :])

                    @pl.when(place >= local)
                    def _():
                        add_slot(other_key, other_value, place - local, mask_s[pl.ds(c, 1), :])

                    return inner

                lax.fori_loop(0, cites, one_cite, 0)
                lane = lax.broadcasted_iota(jnp.int32, (suffix_len, LANES), 1)
                stats = jnp.zeros((suffix_len, LANES), jnp.float32)
                for g in range(heads):
                    part = slice(g * suffix_len, (g + 1) * suffix_len)
                    total = acc_s[part, HD : 2 * HD]
                    out_ref[j, :, g * HD : (g + 1) * HD] = (acc_s[part, 0:HD] / total).astype(jnp.bfloat16)
                    stats = jnp.where(lane % heads == g, max_s[part, :] + jnp.log2(total), stats)
                out_ref[j, :, heads * HD :] = split_level(stats, lane, heads).astype(jnp.bfloat16)

            @pl.when(found < 0)
            def _():
                out_ref[j, :, 0 : heads * HD] = jnp.zeros((suffix_len, heads * HD), jnp.bfloat16)
                lane = lax.broadcasted_iota(jnp.int32, (suffix_len, LANES), 1)
                out_ref[j, :, heads * HD :] = jnp.where(lane < heads, very_low, 0.0).astype(jnp.bfloat16)

            return carry

        lax.fori_loop(0, requests, one_request, 0)


def split_level(level, lane, heads):
    stats = jnp.zeros_like(level)
    for i in range(PARTS):
        piece = level.astype(jnp.bfloat16).astype(jnp.float32)
        stats = jnp.where(lane // heads == i, piece, stats)
        level = level - piece
    return stats


def get_level(tile, heads):
    level = tile.astype(jnp.float32)
    total = level
    for i in range(1, PARTS):
        total = total + pltpu.roll(level, LANES - i * heads, 1)
    return total


def host_kernel(query_ref, fresh_key_ref, fresh_value_ref, suffix_key_ref, suffix_value_ref, out_ref, level_ref):
    suffix_len, width = query_ref.shape
    heads = width // HD
    query = stack_heads(query_ref[...], heads)
    fresh = contract_last(query, fresh_key_ref[...]) * log2_scale
    near = contract_last(query, suffix_key_ref[...]) * log2_scale
    place = lax.broadcasted_iota(jnp.int32, near.shape, 0) % suffix_len
    near = jnp.where(lax.broadcasted_iota(jnp.int32, near.shape, 1) <= place, near, very_low)
    top = jnp.maximum(jnp.max(fresh, axis=1, keepdims=True), jnp.max(near, axis=1, keepdims=True))
    fresh = jnp.exp2(fresh - top)
    near = jnp.exp2(near - top)
    total = jnp.sum(fresh, axis=1, keepdims=True) + jnp.sum(near, axis=1, keepdims=True)
    acc = jnp.dot(fresh.astype(jnp.bfloat16), fresh_value_ref[...], preferred_element_type=jnp.float32)
    acc = acc + jnp.dot(near.astype(jnp.bfloat16), suffix_value_ref[...], preferred_element_type=jnp.float32)
    acc = acc / total
    level = jnp.broadcast_to(top + jnp.log2(total), acc.shape)
    lane = lax.broadcasted_iota(jnp.int32, (suffix_len, LANES), 1)
    levels = jnp.zeros((suffix_len, LANES), jnp.float32)
    for g in range(heads):
        part = slice(g * suffix_len, (g + 1) * suffix_len)
        out_ref[:, g * HD : (g + 1) * HD] = acc[part]
        levels = jnp.where(lane == g, level[part], levels)
    level_ref[...] = levels


def weigh(levels):
    top = functools.reduce(jnp.maximum, levels)
    shares = [jnp.exp2(level - top) for level in levels]
    total = functools.reduce(jnp.add, shares)
    return [share / total for share in shares], top + jnp.log2(total)


def merge_kernel(*refs, packed, wide, wide_out):
    heads = refs[0].shape[-1] // HD - (1 if packed else 0)
    width = heads * HD
    outs = refs[packed + 2 * wide :]
    requests, suffix_len = outs[0].shape[:2]
    lane = lax.broadcasted_iota(jnp.int32, (suffix_len, LANES), 1)
    for j in range(requests):
        bodies = [refs[i] for i in range(packed)] + [refs[packed + 2 * i] for i in range(wide)]
        levels = [get_level(refs[i][j, :, width:], heads) for i in range(packed)]
        levels += [refs[packed + 2 * i + 1][j] for i in range(wide)]
        top = functools.reduce(jnp.maximum, levels)
        shares = [jnp.exp2(level - top) for level in levels]
        total = functools.reduce(jnp.add, shares)
        shares = [share / total for share in shares]
        for g in range(heads):
            part = slice(g * HD, (g + 1) * HD)
            terms = [b[j, :, part].astype(jnp.float32) * w[:, g : g + 1] for b, w in zip(bodies, shares)]
            outs[0][j, :, part] = functools.reduce(jnp.add, terms).astype(outs[0].dtype)
        level = top + jnp.log2(total)
        if wide_out:
            outs[1][j] = level
        elif outs[0].shape[-1] > width:
            spread = level
            for i in range(1, PARTS):
                spread = jnp.where(lane // heads == i, pltpu.roll(level, i * heads, 1), spread)
            outs[0][j, :, width:] = split_level(spread, lane, heads).astype(jnp.bfloat16)


def merge_call(packed, wide, out_shape, name):
    wide_out = isinstance(out_shape, tuple)
    return in_vmem(
        functools.partial(merge_kernel, packed=len(packed), wide=len(wide), wide_out=wide_out),
        out_shape,
        (*packed, *(part for pair in wide for part in pair)),
        name=name,
    )


def in_vmem(kernel, out_shape, operands, scratch=(), smem=0, spaces=None, cost=None, name=None):
    spaces = spaces or [pltpu.SMEM] * smem + [pltpu.VMEM] * (len(operands) - smem)
    many = isinstance(out_shape, tuple)
    return pl.pallas_call(
        kernel,
        out_shape=out_shape,
        in_specs=[pl.BlockSpec(memory_space=s) for s in spaces],
        out_specs=tuple(pl.BlockSpec(memory_space=pltpu.VMEM) for _ in out_shape)
        if many
        else pl.BlockSpec(memory_space=pltpu.VMEM),
        scratch_shapes=list(scratch),
        compiler_params=pltpu.CompilerParams(vmem_limit_bytes=VMEM_BYTES),
        cost_estimate=cost,
        name=name,
    )(*operands)


def shift(value, first, hop):
    pairs = []
    for x in range(RING):
        for y in range(RING):
            for c in range(2):
                along_x = (c == 0) == first
                to_x = (x + hop) % RING if along_x else x
                to_y = y if along_x else (y + hop) % RING
                pairs.append(((x * RING + y) * 2 + c, (to_x * RING + to_y) * 2 + c))
    return lax.ppermute(value, ("x", "y", "c"), pairs)


def attend_call(tables, blocks, caches):
    requests, packed_len, width = blocks[0].shape
    cites = tables[0].shape[1]
    suffix_len, heads = packed_len - cites, width // HD
    rows = suffix_len * heads
    count = len(blocks)
    out = jax.ShapeDtypeStruct((requests, suffix_len, width + LANES), jnp.bfloat16)
    return in_vmem(
        functools.partial(attend_kernel, count=count, suffix_len=suffix_len, heads=heads, cites=cites),
        (out,) * count,
        (*tables, *blocks, *caches),
        scratch=(
            pltpu.VMEM((cites, caches[0].shape[1]), jnp.float32),
            pltpu.VMEM((rows, HD), jnp.bfloat16),
            pltpu.VMEM((rows, LANES), jnp.float32),
            pltpu.VMEM((rows, 2 * HD), jnp.float32),
        ),
        smem=count,
        cost=pl.CostEstimate(
            flops=count * requests * cites * rows * HD * 1024, transcendentals=0, bytes_accessed=count * 16 * 1024 * 1024
        ),
        name="attend_class",
    )


def body(
    queries,
    suffix_keys,
    suffix_values,
    passage_keys,
    passage_values,
    fresh_keys,
    fresh_values,
    citations,
    selected,
):
    _, suffix_len, width = queries.shape
    local_passages, length, _ = passage_keys.shape
    heads = width // HD
    cites = citations.shape[1]
    chip = lax.axis_index("x") * RING + lax.axis_index("y")
    core = lax.axis_index("c")

    packed = in_vmem(
        pack_kernel,
        jax.ShapeDtypeStruct((suffix_len + cites, width), jnp.bfloat16),
        (citations, queries[0], selected[0]),
        scratch=(pltpu.SemaphoreType.DMA,),
        spaces=(pltpu.SMEM, pl.ANY, pltpu.VMEM),
        name="pack",
    )
    packed, passage_keys, passage_values = lax.optimization_barrier((packed, passage_keys, passage_values))
    swap = [(0, 1), (1, 0)]
    other_keys = lax.ppermute(passage_keys, "c", swap)
    other_values = lax.ppermute(passage_values, "c", swap)

    host_out, host_level = in_vmem(
        host_kernel,
        (
            jax.ShapeDtypeStruct((suffix_len, width), jnp.float32),
            jax.ShapeDtypeStruct((suffix_len, LANES), jnp.float32),
        ),
        (
            queries[0],
            fresh_keys.reshape(-1, HD),
            fresh_values.reshape(-1, HD),
            suffix_keys[0],
            suffix_values[0],
        ),
        name="host_part",
    )

    row = in_vmem(
        row_kernel,
        jax.ShapeDtypeStruct((RING, *packed.shape), packed.dtype),
        (packed, *(shift(packed, True, hop) for hop in HOPS[1:])),
        name="row",
    )
    row, host_out, host_level = lax.optimization_barrier((row, host_out, host_level))
    classes = [row] + [shift(row, False, hop) for hop in HOPS[1:]]

    def places(block):
        marks = block[:, suffix_len:, 0].astype(jnp.int32)
        named = jnp.where(marks < 0, -1 - marks, marks)
        local = named - chip * (2 * local_passages)
        here = (local >= 0) & (local < 2 * local_passages)
        return jnp.where(here, (local + core * local_passages) % (2 * local_passages), -1)

    def attend(blocks):
        return attend_call([places(b) for b in blocks], blocks, (passage_keys, passage_values, other_keys, other_values))

    own = attend(classes[0:1])
    near_blocks, own = lax.optimization_barrier((classes[1:3], own))
    near = attend(near_blocks)
    far_block, near = lax.optimization_barrier((classes[3:4], near))
    far = attend(far_block)
    results = list(own) + list(near) + list(far)
    back = [shift(r, False, RING - hop) for r, hop in zip(results[1:], HOPS[1:])]
    partial = merge_call(
        (results[0], *back[:2]),
        (),
        (
            jax.ShapeDtypeStruct((RING, suffix_len, width), jnp.float32),
            jax.ShapeDtypeStruct((RING, suffix_len, LANES), jnp.float32),
        ),
        "merge_near",
    )
    merged = merge_call(
        back[2:], (partial,), jax.ShapeDtypeStruct((RING, suffix_len, width + LANES), jnp.bfloat16), "merge_row"
    )
    home = [merged[j : j + 1] for j in range(RING)]
    home = home[:1] + [shift(h, True, RING - hop) for h, hop in zip(home[1:], HOPS[1:])]
    attended = merge_call(
        home,
        ((host_out[None], host_level[None]),),
        jax.ShapeDtypeStruct((1, suffix_len, width), jnp.bfloat16),
        "merge_home",
    )[0]
    groups = lax.psum(1, "kv")
    pieces = attended.reshape(groups, suffix_len // groups, width)
    pieces = lax.all_to_all(pieces, "kv", split_axis=0, concat_axis=0, tiled=True)
    return jnp.transpose(pieces, (1, 0, 2)).reshape(1, suffix_len // groups, groups * width)


def solution(mesh):
    fine = Mesh(mesh.devices.reshape(RING, RING, 2, -1), ("x", "y", "c", "kv"))
    part = ("x", "y", "c")
    placed = (
        P(part, None, "kv"),
        P(part, None, "kv"),
        P(part, None, "kv"),
        P(part, None, "kv"),
        P(part, None, "kv"),
        P(part, None, None, "kv"),
        P(part, None, None, "kv"),
        P(part, None),
        P(part, None, None),
    )
    return jax.shard_map(body, mesh=fine, in_specs=placed, out_specs=P(part, "kv", None), check_vma=False)
```

```python
import functools
import math

import jax
import jax.numpy as jnp
from jax import lax
from jax.experimental import pallas as pl
from jax.experimental.pallas import tpu as pltpu
from jax.sharding import Mesh
from jax.sharding import PartitionSpec as P

HD = 128
LANES = 128
PARTS = 3
RING = 4
HOPS = (0, 1, 3, 2)
very_low = -1e30
log2_scale = math.log2(math.e) / math.sqrt(HD)
CHUNKS = 2
VMEM_BYTES = 24 * 1024 * 1024


def contract_last(left, right):
    return lax.dot_general(
        left, right, (((1,), (1,)), ((), ())), preferred_element_type=jnp.float32
    )


def stack_heads(rows, heads):
    return jnp.concatenate([rows[:, g * HD : (g + 1) * HD] for g in range(heads)], axis=0)


def pack_kernel(cite_ref, query_ref, picks_ref, out_ref, cite_s, picks_s, sems):
    suffix_len, width = query_ref.shape
    cites, pick_count = picks_ref.shape
    blocks = width // LANES
    copies = (
        pltpu.make_async_copy(picks_ref, picks_s, sems.at[0]),
        pltpu.make_async_copy(cite_ref, cite_s, sems.at[1]),
        pltpu.make_async_copy(query_ref, out_ref.at[pl.ds(0, suffix_len), :], sems.at[2]),
    )
    for copy in copies:
        copy.start()
    copies[0].wait()
    picks = jnp.concatenate([picks_s[c : c + 1, :] for c in range(cites)], axis=1)
    total = cites * pick_count
    within = lax.broadcasted_iota(jnp.int32, (LANES, total), 0)
    low = jnp.where(within == picks % LANES, 1.0, 0.0).astype(jnp.bfloat16)
    row = lax.broadcasted_iota(jnp.int32, (blocks * cites, total), 0)
    owner = lax.broadcasted_iota(jnp.int32, (blocks * cites, total), 1) // pick_count
    high = jnp.where(row == (picks // LANES) * cites + owner, 1.0, 0.0).astype(jnp.bfloat16)
    hits = contract_last(high, low)
    copies[1].wait()
    line = lax.broadcasted_iota(jnp.int32, (cites, LANES), 0)
    ids = jnp.zeros((cites, LANES), jnp.int32)
    for c in range(cites):
        ids = jnp.where(line == c, cite_s[0, c], ids)
    ids = ids.astype(jnp.float32)
    for h in range(blocks):
        hit = hits[h * cites : (h + 1) * cites, :]
        out_ref[suffix_len:, h * LANES : (h + 1) * LANES] = jnp.where(hit > 0.5, -1.0 - ids, ids).astype(jnp.bfloat16)
    copies[2].wait()


def row_kernel(*refs):
    for j, source in enumerate(refs[:-1]):
        refs[-1][j, :, :] = source[...]


def attend_kernel(*refs, count, suffix_len, heads, cites):
    tables, blocks = refs[0:count], refs[count : 2 * count]
    own_key, own_value, other_key, other_value = refs[2 * count : 2 * count + 4]
    outs = refs[2 * count + 4 : 3 * count + 4]
    mask_s, query_s, max_s, acc_s, key_s, value_s, order_s, sems = refs[3 * count + 4 :]
    rows = suffix_len * heads
    chunk = rows // CHUNKS
    requests = blocks[0].shape[0]
    local = own_key.shape[0]

    limit = count * requests * cites
    total = jnp.int32(0)
    for table_ref in tables:
        for i in range(requests * cites):
            place = table_ref[i // cites, i % cites]
            order_s[total] = place
            total = total + jnp.where(place >= 0, 1, 0)

    def copies(place, slot, key_ref, value_ref):
        return (
            pltpu.make_async_copy(key_ref.at[place], key_s.at[slot], sems.at[0, slot]),
            pltpu.make_async_copy(value_ref.at[place], value_s.at[slot], sems.at[1, slot]),
        )

    def fetch(i):
        place, slot = order_s[i], i % 2

        @pl.when(place < local)
        def _():
            for copy in copies(place, slot, own_key, own_value):
                copy.start()

        @pl.when(place >= local)
        def _():
            for copy in copies(place - local, slot, other_key, other_value):
                copy.start()

    @pl.when(total > 0)
    def _():
        fetch(0)

    order_s[limit] = 0

    def add_slot(slot, bias):
        parts = [pl.ds(start, chunk) for start in range(0, rows, chunk)]
        ahead = contract_last(query_s[parts[0], :], key_s[slot])
        for i, part in enumerate(parts):
            scores = ahead * log2_scale + bias
            if i + 1 < len(parts):
                ahead = contract_last(query_s[parts[i + 1], :], key_s[slot])
            old_max = max_s[part, :]
            new_max = jnp.maximum(old_max, jnp.max(scores, axis=1, keepdims=True))
            level = jnp.concatenate([new_max] * (scores.shape[1] // LANES), axis=1)
            weights = jnp.exp2(scores - level).astype(jnp.bfloat16)
            factor = jnp.exp2(old_max - new_max)
            value = value_s[slot]
            value = jnp.concatenate([value, jnp.ones_like(value)], axis=1)
            added = jnp.dot(weights, value, preferred_element_type=jnp.float32)
            acc_s[part, :] = acc_s[part, :] * jnp.concatenate([factor, factor], axis=1) + added
            max_s[part, :] = new_max

    for table_ref, packed_ref, out_ref in zip(tables, blocks, outs):

        def one_request(j, carry, table_ref=table_ref, packed_ref=packed_ref, out_ref=out_ref):
            found = table_ref[j, 0]
            for c in range(1, cites):
                found = jnp.maximum(found, table_ref[j, c])

            @pl.when(found >= 0)
            def _():
                query_s[...] = stack_heads(packed_ref[j, 0:suffix_len, :], heads)
                marks = packed_ref[j, suffix_len : suffix_len + cites, :].astype(jnp.float32)
                mask_s[...] = jnp.where(marks < 0.0, very_low, 0.0)
                max_s[...] = jnp.full_like(max_s, very_low)
                acc_s[...] = jnp.zeros_like(acc_s)

                def one_cite(c, inner):
                    @pl.when(table_ref[j, c] >= 0)
                    def _():
                        i = order_s[limit]
                        order_s[limit] = i + 1
                        for copy in copies(0, i % 2, own_key, own_value):
                            copy.wait()

                        @pl.when(i + 1 < total)
                        def _():
                            fetch(i + 1)

                        add_slot(i % 2, mask_s[pl.ds(c, 1), :])

                    return inner

                lax.fori_loop(0, cites, one_cite, 0)
                lane = lax.broadcasted_iota(jnp.int32, (suffix_len, LANES), 1)
                stats = jnp.zeros((suffix_len, LANES), jnp.float32)
                for g in range(heads):
                    part = slice(g * suffix_len, (g + 1) * suffix_len)
                    total_weight = acc_s[part, HD : 2 * HD]
                    out_ref[j, :, g * HD : (g + 1) * HD] = (acc_s[part, 0:HD] / total_weight).astype(jnp.bfloat16)
                    stats = jnp.where(lane % heads == g, max_s[part, :] + jnp.log2(total_weight), stats)
                out_ref[j, :, heads * HD :] = split_level(stats, lane, heads).astype(jnp.bfloat16)

            @pl.when(found < 0)
            def _():
                out_ref[j, :, 0 : heads * HD] = jnp.zeros((suffix_len, heads * HD), jnp.bfloat16)
                lane = lax.broadcasted_iota(jnp.int32, (suffix_len, LANES), 1)
                out_ref[j, :, heads * HD :] = jnp.where(lane < heads, very_low, 0.0).astype(jnp.bfloat16)

            return carry

        lax.fori_loop(0, requests, one_request, 0)


def split_level(level, lane, heads):
    stats = jnp.zeros_like(level)
    for i in range(PARTS):
        piece = level.astype(jnp.bfloat16).astype(jnp.float32)
        stats = jnp.where(lane // heads == i, piece, stats)
        level = level - piece
    return stats


def get_level(tile, heads):
    level = tile.astype(jnp.float32)
    total = level
    for i in range(1, PARTS):
        total = total + pltpu.roll(level, LANES - i * heads, 1)
    return total


def host_kernel(query_ref, fresh_key_ref, fresh_value_ref, suffix_key_ref, suffix_value_ref, out_ref, level_ref):
    suffix_len, width = query_ref.shape
    heads = width // HD
    query = stack_heads(query_ref[...], heads)
    fresh = contract_last(query, fresh_key_ref[...]) * log2_scale
    near = contract_last(query, suffix_key_ref[...]) * log2_scale
    place = lax.broadcasted_iota(jnp.int32, near.shape, 0) % suffix_len
    near = jnp.where(lax.broadcasted_iota(jnp.int32, near.shape, 1) <= place, near, very_low)
    top = jnp.maximum(jnp.max(fresh, axis=1, keepdims=True), jnp.max(near, axis=1, keepdims=True))
    fresh = jnp.exp2(fresh - top)
    near = jnp.exp2(near - top)
    total = jnp.sum(fresh, axis=1, keepdims=True) + jnp.sum(near, axis=1, keepdims=True)
    acc = jnp.dot(fresh.astype(jnp.bfloat16), fresh_value_ref[...], preferred_element_type=jnp.float32)
    acc = acc + jnp.dot(near.astype(jnp.bfloat16), suffix_value_ref[...], preferred_element_type=jnp.float32)
    acc = acc / total
    level = jnp.broadcast_to(top + jnp.log2(total), acc.shape)
    lane = lax.broadcasted_iota(jnp.int32, (suffix_len, LANES), 1)
    levels = jnp.zeros((suffix_len, LANES), jnp.float32)
    for g in range(heads):
        part = slice(g * suffix_len, (g + 1) * suffix_len)
        out_ref[:, g * HD : (g + 1) * HD] = acc[part]
        levels = jnp.where(lane == g, level[part], levels)
    level_ref[...] = levels


def weigh(levels):
    top = functools.reduce(jnp.maximum, levels)
    shares = [jnp.exp2(level - top) for level in levels]
    total = functools.reduce(jnp.add, shares)
    return [share / total for share in shares], top + jnp.log2(total)


def spread_parts(level, lane, heads):
    wide = level
    for i in range(1, PARTS):
        wide = jnp.where(lane // heads == i, pltpu.roll(level, i * heads, 1), wide)
    return split_level(wide, lane, heads).astype(jnp.bfloat16)


def merge_kernel(*refs, packed, wide, wide_out):
    heads = refs[0].shape[-1] // HD - (1 if packed else 0)
    width = heads * HD
    outs = refs[packed + 2 * wide :]
    requests, suffix_len = outs[0].shape[:2]
    lane = lax.broadcasted_iota(jnp.int32, (suffix_len, LANES), 1)
    part = lax.broadcasted_iota(jnp.int32, (LANES, width), 0)
    head = lax.broadcasted_iota(jnp.int32, (LANES, width), 1) // HD
    widen = jnp.where((part % heads == head) & (part < PARTS * heads), 1.0, 0.0).astype(jnp.bfloat16)
    for j in range(requests):
        bodies = [refs[i] for i in range(packed)] + [refs[packed + 2 * i] for i in range(wide)]
        levels = [get_level(refs[i][j, :, width:], heads) for i in range(packed)]
        levels += [refs[packed + 2 * i + 1][j] for i in range(wide)]
        top = functools.reduce(jnp.maximum, levels)
        shares = [jnp.exp2(level - top) for level in levels]
        total = functools.reduce(jnp.add, shares)
        shares = [share / total for share in shares]
        terms = [
            b[j, :, 0:width].astype(jnp.float32) * jnp.dot(spread_parts(w, lane, heads), widen, preferred_element_type=jnp.float32)
            for b, w in zip(bodies, shares)
        ]
        outs[0][j, :, 0:width] = functools.reduce(jnp.add, terms).astype(outs[0].dtype)
        level = top + jnp.log2(total)
        if wide_out:
            outs[1][j] = level
        elif outs[0].shape[-1] > width:
            outs[0][j, :, width:] = spread_parts(level, lane, heads)


def merge_call(packed, wide, out_shape, name):
    wide_out = isinstance(out_shape, tuple)
    return in_vmem(
        functools.partial(merge_kernel, packed=len(packed), wide=len(wide), wide_out=wide_out),
        out_shape,
        (*packed, *(part for pair in wide for part in pair)),
        name=name,
    )


def in_vmem(kernel, out_shape, operands, scratch=(), smem=0, spaces=None, cost=None, name=None):
    spaces = spaces or [pltpu.SMEM] * smem + [pltpu.VMEM] * (len(operands) - smem)
    many = isinstance(out_shape, tuple)
    return pl.pallas_call(
        kernel,
        out_shape=out_shape,
        in_specs=[pl.BlockSpec(memory_space=s) for s in spaces],
        out_specs=tuple(pl.BlockSpec(memory_space=pltpu.VMEM) for _ in out_shape)
        if many
        else pl.BlockSpec(memory_space=pltpu.VMEM),
        scratch_shapes=list(scratch),
        compiler_params=pltpu.CompilerParams(vmem_limit_bytes=VMEM_BYTES),
        cost_estimate=cost,
        name=name,
    )(*operands)


def shift(value, first, hop):
    pairs = []
    for x in range(RING):
        for y in range(RING):
            for c in range(2):
                along_x = (c == 0) == first
                to_x = (x + hop) % RING if along_x else x
                to_y = y if along_x else (y + hop) % RING
                pairs.append(((x * RING + y) * 2 + c, (to_x * RING + to_y) * 2 + c))
    return lax.ppermute(value, ("x", "y", "c"), pairs)


def attend_call(tables, blocks, caches):
    requests, packed_len, width = blocks[0].shape
    cites = tables[0].shape[1]
    length = caches[0].shape[1]
    suffix_len, heads = packed_len - cites, width // HD
    rows = suffix_len * heads
    count = len(blocks)
    out = jax.ShapeDtypeStruct((requests, suffix_len, width + LANES), jnp.bfloat16)
    return in_vmem(
        functools.partial(attend_kernel, count=count, suffix_len=suffix_len, heads=heads, cites=cites),
        (out,) * count,
        (*tables, *blocks, *(pltpu.with_memory_space_constraint(v, pltpu.HBM) for v in caches)),
        scratch=(
            pltpu.VMEM((cites, length), jnp.float32),
            pltpu.VMEM((rows, HD), jnp.bfloat16),
            pltpu.VMEM((rows, LANES), jnp.float32),
            pltpu.VMEM((rows, 2 * HD), jnp.float32),
            pltpu.VMEM((2, length, HD), jnp.bfloat16),
            pltpu.VMEM((2, length, HD), jnp.bfloat16),
            pltpu.SMEM((count * requests * cites + 1,), jnp.int32),
            pltpu.SemaphoreType.DMA((2, 2)),
        ),
        spaces=(pltpu.SMEM,) * count + (pltpu.VMEM,) * count + (pltpu.HBM,) * len(caches),
        cost=pl.CostEstimate(
            flops=count * requests * cites * rows * HD * length,
            transcendentals=0,
            bytes_accessed=count * 16 * 1024 * 1024,
        ),
        name="attend_class",
    )


def body(
    queries,
    suffix_keys,
    suffix_values,
    passage_keys,
    passage_values,
    fresh_keys,
    fresh_values,
    citations,
    selected,
):
    _, suffix_len, width = queries.shape
    local_passages, length, _ = passage_keys.shape
    heads = width // HD
    cites = citations.shape[1]
    chip = lax.axis_index("x") * RING + lax.axis_index("y")
    core = lax.axis_index("c")

    packed = in_vmem(
        pack_kernel,
        jax.ShapeDtypeStruct((suffix_len + cites, width), jnp.bfloat16),
        tuple(pltpu.with_memory_space_constraint(v, pltpu.HBM) for v in (citations, queries[0], selected[0])),
        scratch=(
            pltpu.SMEM(citations.shape, jnp.int32),
            pltpu.VMEM(selected.shape[1:], jnp.int32),
            pltpu.SemaphoreType.DMA((3,)),
        ),
        spaces=(pltpu.HBM,) * 3,
        name="pack",
    )
    packed, passage_keys, passage_values = lax.optimization_barrier((packed, passage_keys, passage_values))
    swap = [(0, 1), (1, 0)]
    other_keys = lax.ppermute(passage_keys, "c", swap)
    other_values = lax.ppermute(passage_values, "c", swap)

    host_out, host_level = in_vmem(
        host_kernel,
        (
            jax.ShapeDtypeStruct((suffix_len, width), jnp.float32),
            jax.ShapeDtypeStruct((suffix_len, LANES), jnp.float32),
        ),
        (
            queries[0],
            fresh_keys.reshape(-1, HD),
            fresh_values.reshape(-1, HD),
            suffix_keys[0],
            suffix_values[0],
        ),
        name="host_part",
    )

    row = in_vmem(
        row_kernel,
        jax.ShapeDtypeStruct((RING, *packed.shape), packed.dtype),
        (packed, *(shift(packed, True, hop) for hop in HOPS[1:])),
        name="row",
    )
    row, host_out, host_level = lax.optimization_barrier((row, host_out, host_level))
    classes = [row] + [shift(row, False, hop) for hop in HOPS[1:]]

    def places(block):
        marks = block[:, suffix_len:, 0].astype(jnp.int32)
        named = jnp.where(marks < 0, -1 - marks, marks)
        local = named - chip * (2 * local_passages)
        here = (local >= 0) & (local < 2 * local_passages)
        return jnp.where(here, (local + core * local_passages) % (2 * local_passages), -1)

    def attend(blocks):
        return attend_call([places(b) for b in blocks], blocks, (passage_keys, passage_values, other_keys, other_values))

    results = [attend(classes[0:1])[0]]
    for block in classes[1:]:
        block, results[-1] = lax.optimization_barrier((block, results[-1]))
        results.append(attend([block])[0])
    back = [shift(r, False, RING - hop) for r, hop in zip(results[1:], HOPS[1:])]
    partial = merge_call(
        (results[0], *back[:2]),
        (),
        (
            jax.ShapeDtypeStruct((RING, suffix_len, width), jnp.float32),
            jax.ShapeDtypeStruct((RING, suffix_len, LANES), jnp.float32),
        ),
        "merge_near",
    )
    merged = merge_call(
        back[2:], (partial,), jax.ShapeDtypeStruct((RING, suffix_len, width + LANES), jnp.bfloat16), "merge_row"
    )
    home = [merged[j : j + 1] for j in range(RING)]
    home = home[:1] + [shift(h, True, RING - hop) for h, hop in zip(home[1:], HOPS[1:])]
    attended = merge_call(
        home,
        ((host_out[None], host_level[None]),),
        jax.ShapeDtypeStruct((1, suffix_len, width), jnp.bfloat16),
        "merge_home",
    )[0]
    groups = lax.psum(1, "kv")
    pieces = attended.reshape(groups, suffix_len // groups, width)
    pieces = lax.all_to_all(pieces, "kv", split_axis=0, concat_axis=0, tiled=True)
    return jnp.transpose(pieces, (1, 0, 2)).reshape(1, suffix_len // groups, groups * width)


def solution(mesh):
    fine = Mesh(mesh.devices.reshape(RING, RING, 2, -1), ("x", "y", "c", "kv"))
    part = ("x", "y", "c")
    placed = (
        P(part, None, "kv"),
        P(part, None, "kv"),
        P(part, None, "kv"),
        P(part, None, "kv"),
        P(part, None, "kv"),
        P(part, None, None, "kv"),
        P(part, None, None, "kv"),
        P(part, None),
        P(part, None, None),
    )
    return jax.shard_map(body, mesh=fine, in_specs=placed, out_specs=P(part, "kv", None), check_vma=False)
```

```python
import functools
import math

import jax
import jax.numpy as jnp
from jax import lax
from jax.experimental import pallas as pl
from jax.experimental.pallas import tpu as pltpu
from jax.sharding import Mesh
from jax.sharding import PartitionSpec as P

HD = 128
LANES = 128
PARTS = 3
RING = 4
HOPS = (0, 1, 3, 2)
very_low = -1e30
log2_scale = math.log2(math.e) / math.sqrt(HD)
CHUNKS = 2
VMEM_BYTES = 24 * 1024 * 1024


def contract_last(left, right):
    return lax.dot_general(
        left, right, (((1,), (1,)), ((), ())), preferred_element_type=jnp.float32
    )


def stack_heads(rows, heads):
    return jnp.concatenate([rows[:, g * HD : (g + 1) * HD] for g in range(heads)], axis=0)


def pack_kernel(cite_ref, query_ref, picks_ref, out_ref, cite_s, picks_s, sems):
    suffix_len, width = query_ref.shape
    cites, pick_count = picks_ref.shape
    blocks = width // LANES
    copies = (
        pltpu.make_async_copy(picks_ref, picks_s, sems.at[0]),
        pltpu.make_async_copy(cite_ref, cite_s, sems.at[1]),
        pltpu.make_async_copy(query_ref, out_ref.at[pl.ds(0, suffix_len), :], sems.at[2]),
    )
    for copy in copies:
        copy.start()
    copies[0].wait()
    picks = jnp.concatenate([picks_s[c : c + 1, :] for c in range(cites)], axis=1)
    total = cites * pick_count
    within = lax.broadcasted_iota(jnp.int32, (LANES, total), 0)
    low = jnp.where(within == picks % LANES, 1.0, 0.0).astype(jnp.bfloat16)
    row = lax.broadcasted_iota(jnp.int32, (blocks * cites, total), 0)
    owner = lax.broadcasted_iota(jnp.int32, (blocks * cites, total), 1) // pick_count
    high = jnp.where(row == (picks // LANES) * cites + owner, 1.0, 0.0).astype(jnp.bfloat16)
    hits = contract_last(high, low)
    copies[1].wait()
    line = lax.broadcasted_iota(jnp.int32, (cites, LANES), 0)
    ids = jnp.zeros((cites, LANES), jnp.int32)
    for c in range(cites):
        ids = jnp.where(line == c, cite_s[0, c], ids)
    ids = ids.astype(jnp.float32)
    for h in range(blocks):
        hit = hits[h * cites : (h + 1) * cites, :]
        out_ref[suffix_len:, h * LANES : (h + 1) * LANES] = jnp.where(hit > 0.5, -1.0 - ids, ids).astype(jnp.bfloat16)
    copies[2].wait()


def row_kernel(*refs):
    for j, source in enumerate(refs[:-1]):
        refs[-1][j, :, :] = source[...]


def stage_kernel(own_key, own_value, other_key, other_value, key_ref, value_ref, sems):
    local = own_key.shape[0]
    copies = []
    for i, (source, target, start) in enumerate(
        ((own_key, key_ref, 0), (own_value, value_ref, 0), (other_key, key_ref, local), (other_value, value_ref, local))
    ):
        copies.append(pltpu.make_async_copy(source, target.at[pl.ds(start, local)], sems.at[i]))
        copies[-1].start()
    for copy in copies:
        copy.wait()


def attend_kernel(table_ref, packed_ref, key_ref, value_ref, out_ref, mask_s, query_s, max_s, acc_s):
    requests, suffix_len, wide = out_ref.shape
    heads = wide // HD - 1
    cites = packed_ref.shape[1] - suffix_len
    rows = suffix_len * heads
    chunk = rows // CHUNKS
    parts = [pl.ds(start, chunk) for start in range(0, rows, chunk)]

    def add_slot(place, bias):
        ahead = contract_last(query_s[parts[0], :], key_ref[place])
        for i, part in enumerate(parts):
            scores = ahead * log2_scale + bias
            if i + 1 < len(parts):
                ahead = contract_last(query_s[parts[i + 1], :], key_ref[place])
            old_max = max_s[part, :]
            new_max = jnp.maximum(old_max, jnp.max(scores, axis=1, keepdims=True))
            level = jnp.concatenate([new_max] * (scores.shape[1] // LANES), axis=1)
            weights = jnp.exp2(scores - level).astype(jnp.bfloat16)
            factor = jnp.exp2(old_max - new_max)
            value = value_ref[place]
            value = jnp.concatenate([value, jnp.ones_like(value)], axis=1)
            added = jnp.dot(weights, value, preferred_element_type=jnp.float32)
            acc_s[part, :] = acc_s[part, :] * jnp.concatenate([factor, factor], axis=1) + added
            max_s[part, :] = new_max

    lane = lax.broadcasted_iota(jnp.int32, (suffix_len, LANES), 1)

    def one_request(j, carry):
        found = table_ref[j, 0]
        for c in range(1, cites):
            found = jnp.maximum(found, table_ref[j, c])

        @pl.when(found >= 0)
        def _():
            query_s[...] = stack_heads(packed_ref[j, 0:suffix_len, :], heads)
            marks = packed_ref[j, suffix_len : suffix_len + cites, :].astype(jnp.float32)
            mask_s[...] = jnp.where(marks < 0.0, very_low, 0.0)
            max_s[...] = jnp.full_like(max_s, very_low)
            acc_s[...] = jnp.zeros_like(acc_s)

            def one_cite(c, inner):
                place = table_ref[j, c]

                @pl.when(place >= 0)
                def _():
                    add_slot(place, mask_s[pl.ds(c, 1), :])

                return inner

            lax.fori_loop(0, cites, one_cite, 0)
            stats = jnp.zeros((suffix_len, LANES), jnp.float32)
            for g in range(heads):
                part = slice(g * suffix_len, (g + 1) * suffix_len)
                total = acc_s[part, HD : 2 * HD]
                out_ref[j, :, g * HD : (g + 1) * HD] = (acc_s[part, 0:HD] / total).astype(jnp.bfloat16)
                stats = jnp.where(lane % heads == g, max_s[part, :] + jnp.log2(total), stats)
            out_ref[j, :, heads * HD :] = split_level(stats, lane, heads).astype(jnp.bfloat16)

        @pl.when(found < 0)
        def _():
            out_ref[j, :, 0 : heads * HD] = jnp.zeros((suffix_len, heads * HD), jnp.bfloat16)
            out_ref[j, :, heads * HD :] = jnp.where(lane < heads, very_low, 0.0).astype(jnp.bfloat16)

        return carry

    lax.fori_loop(0, requests, one_request, 0)


def split_level(level, lane, heads):
    stats = jnp.zeros_like(level)
    for i in range(PARTS):
        piece = level.astype(jnp.bfloat16).astype(jnp.float32)
        stats = jnp.where(lane // heads == i, piece, stats)
        level = level - piece
    return stats


def get_level(tile, heads):
    level = tile.astype(jnp.float32)
    total = level
    for i in range(1, PARTS):
        total = total + pltpu.roll(level, LANES - i * heads, 1)
    return total


def host_kernel(query_ref, fresh_key_ref, fresh_value_ref, suffix_key_ref, suffix_value_ref, out_ref, level_ref):
    suffix_len, width = query_ref.shape
    heads = width // HD
    query = stack_heads(query_ref[...], heads)
    fresh = contract_last(query, fresh_key_ref[...]) * log2_scale
    near = contract_last(query, suffix_key_ref[...]) * log2_scale
    place = lax.broadcasted_iota(jnp.int32, near.shape, 0) % suffix_len
    near = jnp.where(lax.broadcasted_iota(jnp.int32, near.shape, 1) <= place, near, very_low)
    top = jnp.maximum(jnp.max(fresh, axis=1, keepdims=True), jnp.max(near, axis=1, keepdims=True))
    fresh = jnp.exp2(fresh - top)
    near = jnp.exp2(near - top)
    total = jnp.sum(fresh, axis=1, keepdims=True) + jnp.sum(near, axis=1, keepdims=True)
    acc = jnp.dot(fresh.astype(jnp.bfloat16), fresh_value_ref[...], preferred_element_type=jnp.float32)
    acc = acc + jnp.dot(near.astype(jnp.bfloat16), suffix_value_ref[...], preferred_element_type=jnp.float32)
    acc = acc / total
    level = jnp.broadcast_to(top + jnp.log2(total), acc.shape)
    lane = lax.broadcasted_iota(jnp.int32, (suffix_len, LANES), 1)
    levels = jnp.zeros((suffix_len, LANES), jnp.float32)
    for g in range(heads):
        part = slice(g * suffix_len, (g + 1) * suffix_len)
        out_ref[:, g * HD : (g + 1) * HD] = acc[part]
        levels = jnp.where(lane == g, level[part], levels)
    level_ref[...] = levels


def weigh(levels):
    top = functools.reduce(jnp.maximum, levels)
    shares = [jnp.exp2(level - top) for level in levels]
    total = functools.reduce(jnp.add, shares)
    return [share / total for share in shares], top + jnp.log2(total)


def spread_parts(level, lane, heads):
    wide = level
    for i in range(1, PARTS):
        wide = jnp.where(lane // heads == i, pltpu.roll(level, i * heads, 1), wide)
    return split_level(wide, lane, heads).astype(jnp.bfloat16)


def merge_kernel(*refs, packed, wide, wide_out):
    heads = refs[0].shape[-1] // HD - (1 if packed else 0)
    width = heads * HD
    outs = refs[packed + 2 * wide :]
    requests, suffix_len = outs[0].shape[:2]
    lane = lax.broadcasted_iota(jnp.int32, (suffix_len, LANES), 1)
    part = lax.broadcasted_iota(jnp.int32, (LANES, width), 0)
    head = lax.broadcasted_iota(jnp.int32, (LANES, width), 1) // HD
    widen = jnp.where((part % heads == head) & (part < PARTS * heads), 1.0, 0.0).astype(jnp.bfloat16)
    for j in range(requests):
        bodies = [refs[i] for i in range(packed)] + [refs[packed + 2 * i] for i in range(wide)]
        levels = [get_level(refs[i][j, :, width:], heads) for i in range(packed)]
        levels += [refs[packed + 2 * i + 1][j] for i in range(wide)]
        top = functools.reduce(jnp.maximum, levels)
        shares = [jnp.exp2(level - top) for level in levels]
        total = functools.reduce(jnp.add, shares)
        shares = [share / total for share in shares]
        terms = [
            b[j, :, 0:width].astype(jnp.float32) * jnp.dot(spread_parts(w, lane, heads), widen, preferred_element_type=jnp.float32)
            for b, w in zip(bodies, shares)
        ]
        outs[0][j, :, 0:width] = functools.reduce(jnp.add, terms).astype(outs[0].dtype)
        level = top + jnp.log2(total)
        if wide_out:
            outs[1][j] = level
        elif outs[0].shape[-1] > width:
            outs[0][j, :, width:] = spread_parts(level, lane, heads)


def merge_call(packed, wide, out_shape, name):
    wide_out = isinstance(out_shape, tuple)
    return in_vmem(
        functools.partial(merge_kernel, packed=len(packed), wide=len(wide), wide_out=wide_out),
        out_shape,
        (*packed, *(part for pair in wide for part in pair)),
        name=name,
    )


def in_vmem(kernel, out_shape, operands, scratch=(), smem=0, spaces=None, cost=None, name=None):
    spaces = spaces or [pltpu.SMEM] * smem + [pltpu.VMEM] * (len(operands) - smem)
    many = isinstance(out_shape, tuple)
    return pl.pallas_call(
        kernel,
        out_shape=out_shape,
        in_specs=[pl.BlockSpec(memory_space=s) for s in spaces],
        out_specs=tuple(pl.BlockSpec(memory_space=pltpu.VMEM) for _ in out_shape)
        if many
        else pl.BlockSpec(memory_space=pltpu.VMEM),
        scratch_shapes=list(scratch),
        compiler_params=pltpu.CompilerParams(vmem_limit_bytes=VMEM_BYTES),
        cost_estimate=cost,
        name=name,
    )(*operands)


def shift(value, first, hop):
    pairs = []
    for x in range(RING):
        for y in range(RING):
            for c in range(2):
                along_x = (c == 0) == first
                to_x = (x + hop) % RING if along_x else x
                to_y = y if along_x else (y + hop) % RING
                pairs.append(((x * RING + y) * 2 + c, (to_x * RING + to_y) * 2 + c))
    return lax.ppermute(value, ("x", "y", "c"), pairs)


def attend_call(table, block, keys, values):
    requests, packed_len, width = block.shape
    cites = table.shape[1]
    length = keys.shape[1]
    suffix_len, heads = packed_len - cites, width // HD
    rows = suffix_len * heads
    return in_vmem(
        attend_kernel,
        jax.ShapeDtypeStruct((requests, suffix_len, width + LANES), jnp.bfloat16),
        (table, block, keys, values),
        scratch=(
            pltpu.VMEM((cites, length), jnp.float32),
            pltpu.VMEM((rows, HD), jnp.bfloat16),
            pltpu.VMEM((rows, LANES), jnp.float32),
            pltpu.VMEM((rows, 2 * HD), jnp.float32),
        ),
        smem=1,
        cost=pl.CostEstimate(
            flops=requests * cites * rows * HD * length, transcendentals=0, bytes_accessed=16 * 1024 * 1024
        ),
        name="attend_class",
    )


def body(
    queries,
    suffix_keys,
    suffix_values,
    passage_keys,
    passage_values,
    fresh_keys,
    fresh_values,
    citations,
    selected,
):
    _, suffix_len, width = queries.shape
    local_passages, length, _ = passage_keys.shape
    heads = width // HD
    cites = citations.shape[1]
    chip = lax.axis_index("x") * RING + lax.axis_index("y")
    core = lax.axis_index("c")

    packed = in_vmem(
        pack_kernel,
        jax.ShapeDtypeStruct((suffix_len + cites, width), jnp.bfloat16),
        tuple(pltpu.with_memory_space_constraint(v, pltpu.HBM) for v in (citations, queries[0], selected[0])),
        scratch=(
            pltpu.SMEM(citations.shape, jnp.int32),
            pltpu.VMEM(selected.shape[1:], jnp.int32),
            pltpu.SemaphoreType.DMA((3,)),
        ),
        spaces=(pltpu.HBM,) * 3,
        name="pack",
    )
    packed, passage_keys, passage_values = lax.optimization_barrier((packed, passage_keys, passage_values))
    swap = [(0, 1), (1, 0)]
    other_keys = lax.ppermute(passage_keys, "c", swap)
    other_values = lax.ppermute(passage_values, "c", swap)

    host_out, host_level = in_vmem(
        host_kernel,
        (
            jax.ShapeDtypeStruct((suffix_len, width), jnp.float32),
            jax.ShapeDtypeStruct((suffix_len, LANES), jnp.float32),
        ),
        (
            queries[0],
            fresh_keys.reshape(-1, HD),
            fresh_values.reshape(-1, HD),
            suffix_keys[0],
            suffix_values[0],
        ),
        name="host_part",
    )

    row = in_vmem(
        row_kernel,
        jax.ShapeDtypeStruct((RING, *packed.shape), packed.dtype),
        (packed, *(shift(packed, True, hop) for hop in HOPS[1:])),
        name="row",
    )
    row, host_out, host_level = lax.optimization_barrier((row, host_out, host_level))
    classes = [row] + [shift(row, False, hop) for hop in HOPS[1:]]

    def places(block):
        marks = block[:, suffix_len:, 0].astype(jnp.int32)
        named = jnp.where(marks < 0, -1 - marks, marks)
        local = named - chip * (2 * local_passages)
        here = (local >= 0) & (local < 2 * local_passages)
        return jnp.where(here, (local + core * local_passages) % (2 * local_passages), -1)

    caches = (passage_keys, passage_values, other_keys, other_values)
    both = jax.ShapeDtypeStruct((2 * local_passages, *passage_keys.shape[1:]), passage_keys.dtype)
    keys, values = in_vmem(
        stage_kernel,
        (both, both),
        tuple(pltpu.with_memory_space_constraint(v, pltpu.HBM) for v in caches),
        scratch=(pltpu.SemaphoreType.DMA((4,)),),
        spaces=(pltpu.HBM,) * 4,
        name="stage",
    )
    results = [attend_call(places(row), row, keys, values)]
    for block in classes[1:]:
        block, results[-1] = lax.optimization_barrier((block, results[-1]))
        results.append(attend_call(places(block), block, keys, values))
    back = [shift(r, False, RING - hop) for r, hop in zip(results[1:], HOPS[1:])]
    partial = merge_call(
        (results[0], *back[:2]),
        (),
        (
            jax.ShapeDtypeStruct((RING, suffix_len, width), jnp.float32),
            jax.ShapeDtypeStruct((RING, suffix_len, LANES), jnp.float32),
        ),
        "merge_near",
    )
    merged = merge_call(
        back[2:], (partial,), jax.ShapeDtypeStruct((RING, suffix_len, width + LANES), jnp.bfloat16), "merge_row"
    )
    home = [merged[j : j + 1] for j in range(RING)]
    home = home[:1] + [shift(h, True, RING - hop) for h, hop in zip(home[1:], HOPS[1:])]
    attended = merge_call(
        home,
        ((host_out[None], host_level[None]),),
        jax.ShapeDtypeStruct((1, suffix_len, width), jnp.bfloat16),
        "merge_home",
    )[0]
    groups = lax.psum(1, "kv")
    pieces = attended.reshape(groups, suffix_len // groups, width)
    pieces = lax.all_to_all(pieces, "kv", split_axis=0, concat_axis=0, tiled=True)
    return jnp.transpose(pieces, (1, 0, 2)).reshape(1, suffix_len // groups, groups * width)


def solution(mesh):
    fine = Mesh(mesh.devices.reshape(RING, RING, 2, -1), ("x", "y", "c", "kv"))
    part = ("x", "y", "c")
    placed = (
        P(part, None, "kv"),
        P(part, None, "kv"),
        P(part, None, "kv"),
        P(part, None, "kv"),
        P(part, None, "kv"),
        P(part, None, None, "kv"),
        P(part, None, None, "kv"),
        P(part, None),
        P(part, None, None),
    )
    return jax.shard_map(body, mesh=fine, in_specs=placed, out_specs=P(part, "kv", None), check_vma=False)
```

```python
import functools
import math

import jax
import jax.numpy as jnp
from jax import lax
from jax.experimental import pallas as pl
from jax.experimental.pallas import tpu as pltpu
from jax.sharding import Mesh
from jax.sharding import PartitionSpec as P

HD = 128
LANES = 128
PARTS = 3
RING = 4
HOPS = (0, 1, 3, 2)
very_low = -1e30
log2_scale = math.log2(math.e) / math.sqrt(HD)
CHUNKS = 2
VMEM_BYTES = 24 * 1024 * 1024


def contract_last(left, right):
    return lax.dot_general(
        left, right, (((1,), (1,)), ((), ())), preferred_element_type=jnp.float32
    )


def stack_heads(rows, heads):
    return jnp.concatenate([rows[:, g * HD : (g + 1) * HD] for g in range(heads)], axis=0)


def pack_kernel(cite_ref, query_ref, picks_ref, out_ref, cite_s, picks_s, sems):
    suffix_len, width = query_ref.shape
    cites, pick_count = picks_ref.shape
    blocks = width // LANES
    copies = (
        pltpu.make_async_copy(picks_ref, picks_s, sems.at[0]),
        pltpu.make_async_copy(cite_ref, cite_s, sems.at[1]),
        pltpu.make_async_copy(query_ref, out_ref.at[pl.ds(0, suffix_len), :], sems.at[2]),
    )
    for copy in copies:
        copy.start()
    copies[0].wait()
    picks = jnp.concatenate([picks_s[c : c + 1, :] for c in range(cites)], axis=1)
    total = cites * pick_count
    within = lax.broadcasted_iota(jnp.int32, (LANES, total), 0)
    low = jnp.where(within == picks % LANES, 1.0, 0.0).astype(jnp.bfloat16)
    row = lax.broadcasted_iota(jnp.int32, (blocks * cites, total), 0)
    owner = lax.broadcasted_iota(jnp.int32, (blocks * cites, total), 1) // pick_count
    high = jnp.where(row == (picks // LANES) * cites + owner, 1.0, 0.0).astype(jnp.bfloat16)
    hits = contract_last(high, low)
    copies[1].wait()
    line = lax.broadcasted_iota(jnp.int32, (cites, LANES), 0)
    ids = jnp.zeros((cites, LANES), jnp.int32)
    for c in range(cites):
        ids = jnp.where(line == c, cite_s[0, c], ids)
    ids = ids.astype(jnp.float32)
    for h in range(blocks):
        hit = hits[h * cites : (h + 1) * cites, :]
        out_ref[suffix_len:, h * LANES : (h + 1) * LANES] = jnp.where(hit > 0.5, -1.0 - ids, ids).astype(jnp.bfloat16)
    copies[2].wait()


def row_kernel(*refs):
    for j, source in enumerate(refs[:-1]):
        refs[-1][j, :, :] = source[...]


def stage_kernel(own_key, own_value, other_key, other_value, key_ref, value_ref, sems):
    local = own_key.shape[0]
    copies = []
    for i, (source, target, start) in enumerate(
        ((own_key, key_ref, 0), (own_value, value_ref, 0), (other_key, key_ref, local), (other_value, value_ref, local))
    ):
        copies.append(pltpu.make_async_copy(source, target.at[pl.ds(start, local)], sems.at[i]))
        copies[-1].start()
    for copy in copies:
        copy.wait()


def attend_kernel(table_ref, packed_ref, key_ref, value_ref, out_ref, mask_s, query_s, max_s, acc_s):
    requests, suffix_len, wide = out_ref.shape
    heads = wide // HD - 1
    cites = packed_ref.shape[1] - suffix_len
    rows = suffix_len * heads
    chunk = rows // CHUNKS
    parts = [pl.ds(start, chunk) for start in range(0, rows, chunk)]

    def add_slot(place, bias):
        ahead = contract_last(query_s[parts[0], :], key_ref[place])
        for i, part in enumerate(parts):
            scores = ahead * log2_scale + bias
            if i + 1 < len(parts):
                ahead = contract_last(query_s[parts[i + 1], :], key_ref[place])
            old_max = max_s[part, :]
            new_max = jnp.maximum(old_max, jnp.max(scores, axis=1, keepdims=True))
            level = jnp.concatenate([new_max] * (scores.shape[1] // LANES), axis=1)
            weights = jnp.exp2(scores - level).astype(jnp.bfloat16)
            factor = jnp.exp2(old_max - new_max)
            value = value_ref[place]
            value = jnp.concatenate([value, jnp.ones_like(value)], axis=1)
            added = jnp.dot(weights, value, preferred_element_type=jnp.float32)
            acc_s[part, :] = acc_s[part, :] * jnp.concatenate([factor, factor], axis=1) + added
            max_s[part, :] = new_max

    lane = lax.broadcasted_iota(jnp.int32, (suffix_len, LANES), 1)

    def one_request(j, carry):
        found = table_ref[j, 0]
        for c in range(1, cites):
            found = jnp.maximum(found, table_ref[j, c])

        @pl.when(found >= 0)
        def _():
            query_s[...] = stack_heads(packed_ref[j, 0:suffix_len, :], heads)
            marks = packed_ref[j, suffix_len : suffix_len + cites, :].astype(jnp.float32)
            mask_s[...] = jnp.where(marks < 0.0, very_low, 0.0)
            max_s[...] = jnp.full_like(max_s, very_low)
            acc_s[...] = jnp.zeros_like(acc_s)

            def one_cite(c, inner):
                place = table_ref[j, c]

                @pl.when(place >= 0)
                def _():
                    add_slot(place, mask_s[pl.ds(c, 1), :])

                return inner

            lax.fori_loop(0, cites, one_cite, 0)
            stats = jnp.zeros((suffix_len, LANES), jnp.float32)
            for g in range(heads):
                part = slice(g * suffix_len, (g + 1) * suffix_len)
                total = acc_s[part, HD : 2 * HD]
                out_ref[j, :, g * HD : (g + 1) * HD] = (acc_s[part, 0:HD] / total).astype(jnp.bfloat16)
                stats = jnp.where(lane % heads == g, max_s[part, :] + jnp.log2(total), stats)
            out_ref[j, :, heads * HD :] = split_level(stats, lane, heads).astype(jnp.bfloat16)

        @pl.when(found < 0)
        def _():
            out_ref[j, :, 0 : heads * HD] = jnp.zeros((suffix_len, heads * HD), jnp.bfloat16)
            out_ref[j, :, heads * HD :] = jnp.where(lane < heads, very_low, 0.0).astype(jnp.bfloat16)

        return carry

    lax.fori_loop(0, requests, one_request, 0)


def split_level(level, lane, heads):
    stats = jnp.zeros_like(level)
    for i in range(PARTS):
        piece = level.astype(jnp.bfloat16).astype(jnp.float32)
        stats = jnp.where(lane // heads == i, piece, stats)
        level = level - piece
    return stats


def get_level(tile, heads):
    level = tile.astype(jnp.float32)
    total = level
    for i in range(1, PARTS):
        total = total + pltpu.roll(level, LANES - i * heads, 1)
    return total


def host_kernel(*refs):
    inputs, (out_ref, level_ref), held, sems = refs[0:5], refs[5:7], refs[7:12], refs[12]
    copies = [pltpu.make_async_copy(source, target, sems.at[i]) for i, (source, target) in enumerate(zip(inputs, held))]
    for copy in copies:
        copy.start()
    for copy in copies:
        copy.wait()
    query_ref, fresh_key_ref, fresh_value_ref, suffix_key_ref, suffix_value_ref = held
    suffix_len, width = query_ref.shape
    heads = width // HD
    query = stack_heads(query_ref[...], heads)
    fresh = contract_last(query, fresh_key_ref[...]) * log2_scale
    near = contract_last(query, suffix_key_ref[...]) * log2_scale
    place = lax.broadcasted_iota(jnp.int32, near.shape, 0) % suffix_len
    near = jnp.where(lax.broadcasted_iota(jnp.int32, near.shape, 1) <= place, near, very_low)
    top = jnp.maximum(jnp.max(fresh, axis=1, keepdims=True), jnp.max(near, axis=1, keepdims=True))
    fresh = jnp.exp2(fresh - top)
    near = jnp.exp2(near - top)
    total = jnp.sum(fresh, axis=1, keepdims=True) + jnp.sum(near, axis=1, keepdims=True)
    acc = jnp.dot(fresh.astype(jnp.bfloat16), fresh_value_ref[...], preferred_element_type=jnp.float32)
    acc = acc + jnp.dot(near.astype(jnp.bfloat16), suffix_value_ref[...], preferred_element_type=jnp.float32)
    acc = acc / total
    level = jnp.broadcast_to(top + jnp.log2(total), acc.shape)
    lane = lax.broadcasted_iota(jnp.int32, (suffix_len, LANES), 1)
    levels = jnp.zeros((suffix_len, LANES), jnp.float32)
    for g in range(heads):
        part = slice(g * suffix_len, (g + 1) * suffix_len)
        out_ref[:, g * HD : (g + 1) * HD] = acc[part]
        levels = jnp.where(lane == g, level[part], levels)
    level_ref[...] = levels


def weigh(levels):
    top = functools.reduce(jnp.maximum, levels)
    shares = [jnp.exp2(level - top) for level in levels]
    total = functools.reduce(jnp.add, shares)
    return [share / total for share in shares], top + jnp.log2(total)


def spread_parts(level, lane, heads):
    wide = level
    for i in range(1, PARTS):
        wide = jnp.where(lane // heads == i, pltpu.roll(level, i * heads, 1), wide)
    return split_level(wide, lane, heads).astype(jnp.bfloat16)


def merge_kernel(*refs, packed, wide, wide_out):
    heads = refs[0].shape[-1] // HD - (1 if packed else 0)
    width = heads * HD
    outs = refs[packed + 2 * wide :]
    requests, suffix_len = outs[0].shape[:2]
    lane = lax.broadcasted_iota(jnp.int32, (suffix_len, LANES), 1)
    part = lax.broadcasted_iota(jnp.int32, (LANES, width), 0)
    head = lax.broadcasted_iota(jnp.int32, (LANES, width), 1) // HD
    widen = jnp.where((part % heads == head) & (part < PARTS * heads), 1.0, 0.0).astype(jnp.bfloat16)
    for j in range(requests):
        bodies = [refs[i] for i in range(packed)] + [refs[packed + 2 * i] for i in range(wide)]
        levels = [get_level(refs[i][j, :, width:], heads) for i in range(packed)]
        levels += [refs[packed + 2 * i + 1][j] for i in range(wide)]
        top = functools.reduce(jnp.maximum, levels)
        shares = [jnp.exp2(level - top) for level in levels]
        total = functools.reduce(jnp.add, shares)
        shares = [share / total for share in shares]
        terms = [
            b[j, :, 0:width].astype(jnp.float32) * jnp.dot(spread_parts(w, lane, heads), widen, preferred_element_type=jnp.float32)
            for b, w in zip(bodies, shares)
        ]
        outs[0][j, :, 0:width] = functools.reduce(jnp.add, terms).astype(outs[0].dtype)
        level = top + jnp.log2(total)
        if wide_out:
            outs[1][j] = level
        elif outs[0].shape[-1] > width:
            outs[0][j, :, width:] = spread_parts(level, lane, heads)


def merge_call(packed, wide, out_shape, name):
    wide_out = isinstance(out_shape, tuple)
    return in_vmem(
        functools.partial(merge_kernel, packed=len(packed), wide=len(wide), wide_out=wide_out),
        out_shape,
        (*packed, *(part for pair in wide for part in pair)),
        name=name,
    )


def in_vmem(kernel, out_shape, operands, scratch=(), smem=0, spaces=None, cost=None, name=None):
    spaces = spaces or [pltpu.SMEM] * smem + [pltpu.VMEM] * (len(operands) - smem)
    many = isinstance(out_shape, tuple)
    return pl.pallas_call(
        kernel,
        out_shape=out_shape,
        in_specs=[pl.BlockSpec(memory_space=s) for s in spaces],
        out_specs=tuple(pl.BlockSpec(memory_space=pltpu.VMEM) for _ in out_shape)
        if many
        else pl.BlockSpec(memory_space=pltpu.VMEM),
        scratch_shapes=list(scratch),
        compiler_params=pltpu.CompilerParams(vmem_limit_bytes=VMEM_BYTES),
        cost_estimate=cost,
        name=name,
    )(*operands)


def shift(value, first, hop):
    pairs = []
    for x in range(RING):
        for y in range(RING):
            for c in range(2):
                along_x = (c == 0) == first
                to_x = (x + hop) % RING if along_x else x
                to_y = y if along_x else (y + hop) % RING
                pairs.append(((x * RING + y) * 2 + c, (to_x * RING + to_y) * 2 + c))
    return lax.ppermute(value, ("x", "y", "c"), pairs)


def attend_call(table, block, keys, values):
    requests, packed_len, width = block.shape
    cites = table.shape[1]
    length = keys.shape[1]
    suffix_len, heads = packed_len - cites, width // HD
    rows = suffix_len * heads
    return in_vmem(
        attend_kernel,
        jax.ShapeDtypeStruct((requests, suffix_len, width + LANES), jnp.bfloat16),
        (table, block, keys, values),
        scratch=(
            pltpu.VMEM((cites, length), jnp.float32),
            pltpu.VMEM((rows, HD), jnp.bfloat16),
            pltpu.VMEM((rows, LANES), jnp.float32),
            pltpu.VMEM((rows, 2 * HD), jnp.float32),
        ),
        smem=1,
        cost=pl.CostEstimate(
            flops=requests * cites * rows * HD * length, transcendentals=0, bytes_accessed=16 * 1024 * 1024
        ),
        name="attend_class",
    )


def body(
    queries,
    suffix_keys,
    suffix_values,
    passage_keys,
    passage_values,
    fresh_keys,
    fresh_values,
    citations,
    selected,
):
    _, suffix_len, width = queries.shape
    local_passages, length, _ = passage_keys.shape
    heads = width // HD
    cites = citations.shape[1]
    chip = lax.axis_index("x") * RING + lax.axis_index("y")
    core = lax.axis_index("c")

    packed = in_vmem(
        pack_kernel,
        jax.ShapeDtypeStruct((suffix_len + cites, width), jnp.bfloat16),
        tuple(pltpu.with_memory_space_constraint(v, pltpu.HBM) for v in (citations, queries[0], selected[0])),
        scratch=(
            pltpu.SMEM(citations.shape, jnp.int32),
            pltpu.VMEM(selected.shape[1:], jnp.int32),
            pltpu.SemaphoreType.DMA((3,)),
        ),
        spaces=(pltpu.HBM,) * 3,
        name="pack",
    )
    packed, passage_keys, passage_values = lax.optimization_barrier((packed, passage_keys, passage_values))
    swap = [(0, 1), (1, 0)]
    other_keys = lax.ppermute(passage_keys, "c", swap)
    other_values = lax.ppermute(passage_values, "c", swap)

    host_inputs = (
        queries[0],
        fresh_keys.reshape(-1, HD),
        fresh_values.reshape(-1, HD),
        suffix_keys[0],
        suffix_values[0],
    )
    host_out, host_level = in_vmem(
        host_kernel,
        (
            jax.ShapeDtypeStruct((suffix_len, width), jnp.float32),
            jax.ShapeDtypeStruct((suffix_len, LANES), jnp.float32),
        ),
        tuple(pltpu.with_memory_space_constraint(v, pltpu.HBM) for v in host_inputs),
        scratch=tuple(pltpu.VMEM(v.shape, v.dtype) for v in host_inputs) + (pltpu.SemaphoreType.DMA((5,)),),
        spaces=(pltpu.HBM,) * 5,
        name="host_part",
    )

    row = in_vmem(
        row_kernel,
        jax.ShapeDtypeStruct((RING, *packed.shape), packed.dtype),
        (packed, *(shift(packed, True, hop) for hop in HOPS[1:])),
        name="row",
    )
    row, host_out, host_level = lax.optimization_barrier((row, host_out, host_level))
    classes = [row] + [shift(row, False, hop) for hop in HOPS[1:]]

    def places(block):
        marks = block[:, suffix_len:, 0].astype(jnp.int32)
        named = jnp.where(marks < 0, -1 - marks, marks)
        local = named - chip * (2 * local_passages)
        here = (local >= 0) & (local < 2 * local_passages)
        return jnp.where(here, (local + core * local_passages) % (2 * local_passages), -1)

    caches = (passage_keys, passage_values, other_keys, other_values)
    both = jax.ShapeDtypeStruct((2 * local_passages, *passage_keys.shape[1:]), passage_keys.dtype)
    keys, values = in_vmem(
        stage_kernel,
        (both, both),
        tuple(pltpu.with_memory_space_constraint(v, pltpu.HBM) for v in caches),
        scratch=(pltpu.SemaphoreType.DMA((4,)),),
        spaces=(pltpu.HBM,) * 4,
        name="stage",
    )
    results = [attend_call(places(row), row, keys, values)]
    for block in classes[1:]:
        block, results[-1] = lax.optimization_barrier((block, results[-1]))
        results.append(attend_call(places(block), block, keys, values))
    back = [shift(r, False, RING - hop) for r, hop in zip(results[1:], HOPS[1:])]
    partial = merge_call(
        (results[0], *back[:2]),
        (),
        (
            jax.ShapeDtypeStruct((RING, suffix_len, width), jnp.float32),
            jax.ShapeDtypeStruct((RING, suffix_len, LANES), jnp.float32),
        ),
        "merge_near",
    )
    merged = merge_call(
        back[2:], (partial,), jax.ShapeDtypeStruct((RING, suffix_len, width + LANES), jnp.bfloat16), "merge_row"
    )
    home = [merged[j : j + 1] for j in range(RING)]
    home = home[:1] + [shift(h, True, RING - hop) for h, hop in zip(home[1:], HOPS[1:])]
    attended = merge_call(
        home,
        ((host_out[None], host_level[None]),),
        jax.ShapeDtypeStruct((1, suffix_len, width), jnp.bfloat16),
        "merge_home",
    )[0]
    groups = lax.psum(1, "kv")
    pieces = attended.reshape(groups, suffix_len // groups, width)
    pieces = lax.all_to_all(pieces, "kv", split_axis=0, concat_axis=0, tiled=True)
    return jnp.transpose(pieces, (1, 0, 2)).reshape(1, suffix_len // groups, groups * width)


def solution(mesh):
    fine = Mesh(mesh.devices.reshape(RING, RING, 2, -1), ("x", "y", "c", "kv"))
    part = ("x", "y", "c")
    placed = (
        P(part, None, "kv"),
        P(part, None, "kv"),
        P(part, None, "kv"),
        P(part, None, "kv"),
        P(part, None, "kv"),
        P(part, None, None, "kv"),
        P(part, None, None, "kv"),
        P(part, None),
        P(part, None, None),
    )
    return jax.shard_map(body, mesh=fine, in_specs=placed, out_specs=P(part, "kv", None), check_vma=False)
```

```python
import functools
import math

import jax
import jax.numpy as jnp
from jax import lax
from jax.experimental import pallas as pl
from jax.experimental.pallas import tpu as pltpu
from jax.sharding import Mesh
from jax.sharding import PartitionSpec as P

HD = 128
LANES = 128
PARTS = 3
RING = 4
HOPS = (0, 1, 3, 2)
very_low = -1e30
log2_scale = math.log2(math.e) / math.sqrt(HD)
CHUNKS = 2
VMEM_BYTES = 24 * 1024 * 1024


def contract_last(left, right):
    return lax.dot_general(
        left, right, (((1,), (1,)), ((), ())), preferred_element_type=jnp.float32
    )


def stack_heads(rows, heads):
    return jnp.concatenate([rows[:, g * HD : (g + 1) * HD] for g in range(heads)], axis=0)


def pack_kernel(cite_ref, query_ref, picks_ref, out_ref, cite_s, picks_s, sems):
    suffix_len, width = query_ref.shape
    cites, pick_count = picks_ref.shape
    blocks = width // LANES
    copies = (
        pltpu.make_async_copy(picks_ref, picks_s, sems.at[0]),
        pltpu.make_async_copy(cite_ref, cite_s, sems.at[1]),
        pltpu.make_async_copy(query_ref, out_ref.at[pl.ds(0, suffix_len), :], sems.at[2]),
    )
    for copy in copies:
        copy.start()
    copies[0].wait()
    picks = jnp.concatenate([picks_s[c : c + 1, :] for c in range(cites)], axis=1)
    total = cites * pick_count
    within = lax.broadcasted_iota(jnp.int32, (LANES, total), 0)
    low = jnp.where(within == picks % LANES, 1.0, 0.0).astype(jnp.bfloat16)
    row = lax.broadcasted_iota(jnp.int32, (blocks * cites, total), 0)
    owner = lax.broadcasted_iota(jnp.int32, (blocks * cites, total), 1) // pick_count
    high = jnp.where(row == (picks // LANES) * cites + owner, 1.0, 0.0).astype(jnp.bfloat16)
    hits = contract_last(high, low)
    copies[1].wait()
    line = lax.broadcasted_iota(jnp.int32, (cites, LANES), 0)
    ids = jnp.zeros((cites, LANES), jnp.int32)
    for c in range(cites):
        ids = jnp.where(line == c, cite_s[0, c], ids)
    ids = ids.astype(jnp.float32)
    for h in range(blocks):
        hit = hits[h * cites : (h + 1) * cites, :]
        out_ref[suffix_len:, h * LANES : (h + 1) * LANES] = jnp.where(hit > 0.5, -1.0 - ids, ids).astype(jnp.bfloat16)
    copies[2].wait()


def row_kernel(*refs):
    for j, source in enumerate(refs[:-1]):
        refs[-1][j, :, :] = source[...]


def stage_kernel(own_key, own_value, other_key, other_value, key_ref, value_ref, sems):
    local = own_key.shape[0]
    copies = []
    for i, (source, target, start) in enumerate(
        ((own_key, key_ref, 0), (own_value, value_ref, 0), (other_key, key_ref, local), (other_value, value_ref, local))
    ):
        copies.append(pltpu.make_async_copy(source, target.at[pl.ds(start, local)], sems.at[i]))
        copies[-1].start()
    for copy in copies:
        copy.wait()


def attend_kernel(table_ref, packed_ref, key_ref, value_ref, out_ref, mask_s, query_s, max_s, acc_s):
    requests, suffix_len, wide = out_ref.shape
    heads = wide // HD - 1
    cites = packed_ref.shape[1] - suffix_len
    rows = suffix_len * heads
    chunk = rows // CHUNKS
    parts = [pl.ds(start, chunk) for start in range(0, rows, chunk)]

    def add_slot(place, bias):
        ahead = contract_last(query_s[parts[0], :], key_ref[place])
        for i, part in enumerate(parts):
            scores = ahead * log2_scale + bias
            if i + 1 < len(parts):
                ahead = contract_last(query_s[parts[i + 1], :], key_ref[place])
            old_max = max_s[part, :]
            new_max = jnp.maximum(old_max, jnp.max(scores, axis=1, keepdims=True))
            level = jnp.concatenate([new_max] * (scores.shape[1] // LANES), axis=1)
            weights = jnp.exp2(scores - level).astype(jnp.bfloat16)
            factor = jnp.exp2(old_max - new_max)
            value = value_ref[place]
            value = jnp.concatenate([value, jnp.ones_like(value)], axis=1)
            added = jnp.dot(weights, value, preferred_element_type=jnp.float32)
            acc_s[part, :] = acc_s[part, :] * jnp.concatenate([factor, factor], axis=1) + added
            max_s[part, :] = new_max

    lane = lax.broadcasted_iota(jnp.int32, (suffix_len, LANES), 1)

    def one_request(j, carry):
        found = table_ref[j, 0]
        for c in range(1, cites):
            found = jnp.maximum(found, table_ref[j, c])

        @pl.when(found >= 0)
        def _():
            query_s[...] = stack_heads(packed_ref[j, 0:suffix_len, :], heads)
            marks = packed_ref[j, suffix_len : suffix_len + cites, :].astype(jnp.float32)
            mask_s[...] = jnp.where(marks < 0.0, very_low, 0.0)
            max_s[...] = jnp.full_like(max_s, very_low)
            acc_s[...] = jnp.zeros_like(acc_s)

            def one_cite(c, inner):
                place = table_ref[j, c]

                @pl.when(place >= 0)
                def _():
                    add_slot(place, mask_s[pl.ds(c, 1), :])

                return inner

            lax.fori_loop(0, cites, one_cite, 0)
            stats = jnp.zeros((suffix_len, LANES), jnp.float32)
            for g in range(heads):
                part = slice(g * suffix_len, (g + 1) * suffix_len)
                total = acc_s[part, HD : 2 * HD]
                out_ref[j, :, g * HD : (g + 1) * HD] = (acc_s[part, 0:HD] / total).astype(jnp.bfloat16)
                stats = jnp.where(lane % heads == g, max_s[part, :] + jnp.log2(total), stats)
            out_ref[j, :, heads * HD :] = split_level(stats, lane, heads).astype(jnp.bfloat16)

        @pl.when(found < 0)
        def _():
            out_ref[j, :, 0 : heads * HD] = jnp.zeros((suffix_len, heads * HD), jnp.bfloat16)
            out_ref[j, :, heads * HD :] = jnp.where(lane < heads, very_low, 0.0).astype(jnp.bfloat16)

        return carry

    lax.fori_loop(0, requests, one_request, 0)


def split_level(level, lane, heads):
    stats = jnp.zeros_like(level)
    for i in range(PARTS):
        piece = level.astype(jnp.bfloat16).astype(jnp.float32)
        stats = jnp.where(lane // heads == i, piece, stats)
        level = level - piece
    return stats


def get_level(tile, heads):
    level = tile.astype(jnp.float32)
    total = level
    for i in range(1, PARTS):
        total = total + pltpu.roll(level, LANES - i * heads, 1)
    return total


def host_kernel(*refs):
    inputs, (out_ref, level_ref), held, sems = refs[0:5], refs[5:7], refs[7:12], refs[12]
    copies = [pltpu.make_async_copy(source, target, sems.at[i]) for i, (source, target) in enumerate(zip(inputs, held))]
    for copy in copies:
        copy.start()
    for copy in copies:
        copy.wait()
    query_ref, fresh_key_ref, fresh_value_ref, suffix_key_ref, suffix_value_ref = held
    suffix_len, width = query_ref.shape
    heads = width // HD
    query = stack_heads(query_ref[...], heads)
    fresh = contract_last(query, fresh_key_ref[...]) * log2_scale
    near = contract_last(query, suffix_key_ref[...]) * log2_scale
    place = lax.broadcasted_iota(jnp.int32, near.shape, 0) % suffix_len
    near = jnp.where(lax.broadcasted_iota(jnp.int32, near.shape, 1) <= place, near, very_low)
    top = jnp.maximum(jnp.max(fresh, axis=1, keepdims=True), jnp.max(near, axis=1, keepdims=True))
    fresh = jnp.exp2(fresh - top)
    near = jnp.exp2(near - top)
    total = jnp.sum(fresh, axis=1, keepdims=True) + jnp.sum(near, axis=1, keepdims=True)
    acc = jnp.dot(fresh.astype(jnp.bfloat16), fresh_value_ref[...], preferred_element_type=jnp.float32)
    acc = acc + jnp.dot(near.astype(jnp.bfloat16), suffix_value_ref[...], preferred_element_type=jnp.float32)
    acc = acc / total
    level = jnp.broadcast_to(top + jnp.log2(total), acc.shape)
    lane = lax.broadcasted_iota(jnp.int32, (suffix_len, LANES), 1)
    levels = jnp.zeros((suffix_len, LANES), jnp.float32)
    for g in range(heads):
        part = slice(g * suffix_len, (g + 1) * suffix_len)
        out_ref[:, g * HD : (g + 1) * HD] = acc[part]
        levels = jnp.where(lane == g, level[part], levels)
    level_ref[...] = levels


def weigh(levels):
    top = functools.reduce(jnp.maximum, levels)
    shares = [jnp.exp2(level - top) for level in levels]
    total = functools.reduce(jnp.add, shares)
    return [share / total for share in shares], top + jnp.log2(total)


def spread_parts(level, lane, heads):
    wide = level
    for i in range(1, PARTS):
        wide = jnp.where(lane // heads == i, pltpu.roll(level, i * heads, 1), wide)
    return split_level(wide, lane, heads).astype(jnp.bfloat16)


def merge_kernel(*refs, packed, wide, wide_out):
    heads = refs[0].shape[-1] // HD - (1 if packed else 0)
    width = heads * HD
    outs = refs[packed + 2 * wide :]
    requests, suffix_len = outs[0].shape[:2]
    lane = lax.broadcasted_iota(jnp.int32, (suffix_len, LANES), 1)
    part = lax.broadcasted_iota(jnp.int32, (LANES, width), 0)
    head = lax.broadcasted_iota(jnp.int32, (LANES, width), 1) // HD
    widen = jnp.where((part % heads == head) & (part < PARTS * heads), 1.0, 0.0).astype(jnp.bfloat16)
    for j in range(requests):
        bodies = [refs[i] for i in range(packed)] + [refs[packed + 2 * i] for i in range(wide)]
        levels = [get_level(refs[i][j, :, width:], heads) for i in range(packed)]
        levels += [refs[packed + 2 * i + 1][j] for i in range(wide)]
        top = functools.reduce(jnp.maximum, levels)
        shares = [jnp.exp2(level - top) for level in levels]
        total = functools.reduce(jnp.add, shares)
        shares = [share / total for share in shares]
        terms = [
            b[j, :, 0:width].astype(jnp.float32) * jnp.dot(spread_parts(w, lane, heads), widen, preferred_element_type=jnp.float32)
            for b, w in zip(bodies, shares)
        ]
        outs[0][j, :, 0:width] = functools.reduce(jnp.add, terms).astype(outs[0].dtype)
        level = top + jnp.log2(total)
        if wide_out:
            outs[1][j] = level
        elif outs[0].shape[-1] > width:
            outs[0][j, :, width:] = spread_parts(level, lane, heads)


def merge_call(packed, wide, out_shape, name):
    wide_out = isinstance(out_shape, tuple)
    return in_vmem(
        functools.partial(merge_kernel, packed=len(packed), wide=len(wide), wide_out=wide_out),
        out_shape,
        (*packed, *(part for pair in wide for part in pair)),
        name=name,
    )


def in_vmem(kernel, out_shape, operands, scratch=(), smem=0, spaces=None, cost=None, name=None):
    spaces = spaces or [pltpu.SMEM] * smem + [pltpu.VMEM] * (len(operands) - smem)
    many = isinstance(out_shape, tuple)
    return pl.pallas_call(
        kernel,
        out_shape=out_shape,
        in_specs=[pl.BlockSpec(memory_space=s) for s in spaces],
        out_specs=tuple(pl.BlockSpec(memory_space=pltpu.VMEM) for _ in out_shape)
        if many
        else pl.BlockSpec(memory_space=pltpu.VMEM),
        scratch_shapes=list(scratch),
        compiler_params=pltpu.CompilerParams(vmem_limit_bytes=VMEM_BYTES),
        cost_estimate=cost,
        name=name,
    )(*operands)


def shift(value, first, hop):
    pairs = []
    for x in range(RING):
        for y in range(RING):
            for c in range(2):
                along_x = (c == 0) == first
                to_x = (x + hop) % RING if along_x else x
                to_y = y if along_x else (y + hop) % RING
                pairs.append(((x * RING + y) * 2 + c, (to_x * RING + to_y) * 2 + c))
    return lax.ppermute(value, ("x", "y", "c"), pairs)


def attend_call(table, block, keys, values):
    requests, packed_len, width = block.shape
    cites = table.shape[1]
    length = keys.shape[1]
    suffix_len, heads = packed_len - cites, width // HD
    rows = suffix_len * heads
    return in_vmem(
        attend_kernel,
        jax.ShapeDtypeStruct((requests, suffix_len, width + LANES), jnp.bfloat16),
        (table, block, keys, values),
        scratch=(
            pltpu.VMEM((cites, length), jnp.float32),
            pltpu.VMEM((rows, HD), jnp.bfloat16),
            pltpu.VMEM((rows, LANES), jnp.float32),
            pltpu.VMEM((rows, 2 * HD), jnp.float32),
        ),
        smem=1,
        cost=pl.CostEstimate(
            flops=requests * cites * rows * HD * length, transcendentals=0, bytes_accessed=16 * 1024 * 1024
        ),
        name="attend_class",
    )


def body(
    queries,
    suffix_keys,
    suffix_values,
    passage_keys,
    passage_values,
    fresh_keys,
    fresh_values,
    citations,
    selected,
):
    _, suffix_len, width = queries.shape
    local_passages, length, _ = passage_keys.shape
    heads = width // HD
    cites = citations.shape[1]
    chip = lax.axis_index("x") * RING + lax.axis_index("y")
    core = lax.axis_index("c")

    packed = in_vmem(
        pack_kernel,
        jax.ShapeDtypeStruct((suffix_len + cites, width), jnp.bfloat16),
        tuple(pltpu.with_memory_space_constraint(v, pltpu.HBM) for v in (citations, queries[0], selected[0])),
        scratch=(
            pltpu.SMEM(citations.shape, jnp.int32),
            pltpu.VMEM(selected.shape[1:], jnp.int32),
            pltpu.SemaphoreType.DMA((3,)),
        ),
        spaces=(pltpu.HBM,) * 3,
        name="pack",
    )
    swap = [(0, 1), (1, 0)]
    other_keys = lax.ppermute(passage_keys, "c", swap)
    other_values = lax.ppermute(passage_values, "c", swap)

    host_inputs = (
        queries[0],
        fresh_keys.reshape(-1, HD),
        fresh_values.reshape(-1, HD),
        suffix_keys[0],
        suffix_values[0],
    )
    host_out, host_level = in_vmem(
        host_kernel,
        (
            jax.ShapeDtypeStruct((suffix_len, width), jnp.float32),
            jax.ShapeDtypeStruct((suffix_len, LANES), jnp.float32),
        ),
        tuple(pltpu.with_memory_space_constraint(v, pltpu.HBM) for v in host_inputs),
        scratch=tuple(pltpu.VMEM(v.shape, v.dtype) for v in host_inputs) + (pltpu.SemaphoreType.DMA((5,)),),
        spaces=(pltpu.HBM,) * 5,
        name="host_part",
    )

    row = in_vmem(
        row_kernel,
        jax.ShapeDtypeStruct((RING, *packed.shape), packed.dtype),
        (packed, *(shift(packed, True, hop) for hop in HOPS[1:])),
        name="row",
    )
    row, host_out, host_level = lax.optimization_barrier((row, host_out, host_level))
    classes = [row] + [shift(row, False, hop) for hop in HOPS[1:]]

    def places(block):
        marks = block[:, suffix_len:, 0].astype(jnp.int32)
        named = jnp.where(marks < 0, -1 - marks, marks)
        local = named - chip * (2 * local_passages)
        here = (local >= 0) & (local < 2 * local_passages)
        return jnp.where(here, (local + core * local_passages) % (2 * local_passages), -1)

    caches = (passage_keys, passage_values, other_keys, other_values)
    both = jax.ShapeDtypeStruct((2 * local_passages, *passage_keys.shape[1:]), passage_keys.dtype)
    keys, values = in_vmem(
        stage_kernel,
        (both, both),
        tuple(v if v is other_keys else pltpu.with_memory_space_constraint(v, pltpu.HBM) for v in caches),
        scratch=(pltpu.SemaphoreType.DMA((4,)),),
        spaces=(pltpu.HBM, pltpu.HBM, pl.ANY, pltpu.HBM),
        name="stage",
    )
    results = [attend_call(places(row), row, keys, values)]
    for block in classes[1:]:
        block, results[-1] = lax.optimization_barrier((block, results[-1]))
        results.append(attend_call(places(block), block, keys, values))
    back = [shift(r, False, RING - hop) for r, hop in zip(results[1:], HOPS[1:])]
    partial = merge_call(
        (results[0], *back[:2]),
        (),
        (
            jax.ShapeDtypeStruct((RING, suffix_len, width), jnp.float32),
            jax.ShapeDtypeStruct((RING, suffix_len, LANES), jnp.float32),
        ),
        "merge_near",
    )
    merged = merge_call(
        back[2:], (partial,), jax.ShapeDtypeStruct((RING, suffix_len, width + LANES), jnp.bfloat16), "merge_row"
    )
    home = [merged[j : j + 1] for j in range(RING)]
    home = home[:1] + [shift(h, True, RING - hop) for h, hop in zip(home[1:], HOPS[1:])]
    attended = merge_call(
        home,
        ((host_out[None], host_level[None]),),
        jax.ShapeDtypeStruct((1, suffix_len, width), jnp.bfloat16),
        "merge_home",
    )[0]
    groups = lax.psum(1, "kv")
    pieces = attended.reshape(groups, suffix_len // groups, width)
    pieces = lax.all_to_all(pieces, "kv", split_axis=0, concat_axis=0, tiled=True)
    return jnp.transpose(pieces, (1, 0, 2)).reshape(1, suffix_len // groups, groups * width)


def solution(mesh):
    fine = Mesh(mesh.devices.reshape(RING, RING, 2, -1), ("x", "y", "c", "kv"))
    part = ("x", "y", "c")
    placed = (
        P(part, None, "kv"),
        P(part, None, "kv"),
        P(part, None, "kv"),
        P(part, None, "kv"),
        P(part, None, "kv"),
        P(part, None, None, "kv"),
        P(part, None, None, "kv"),
        P(part, None),
        P(part, None, None),
    )
    return jax.shard_map(body, mesh=fine, in_specs=placed, out_specs=P(part, "kv", None), check_vma=False)
```
